512 devices in a mesh: rep: 16 (over y, core), lab: 32 (over x, z).
Axes of the slice: x: 4, y: 8, z: 8, core: 2. Of those that a mesh axis runs over, the one named last changes fastest.
Arguments:
- queries: bfloat16 [65536, 768], P(('rep', 'lab')), may hold values from -6 to 6
- shortlist: int32 [65536, 8], P(('rep', 'lab')), may hold values from 0 to 255, all different within a row; in each aligned block of 128 rows (0 to 127, 128 to 255, ...) at most 8 rows name the same one
- positive: int32 [65536, 8], P(('rep', 'lab')), may hold values from 0 to 255
- label_weight: bfloat16 [32768, 768], P('lab'), may hold values from -0.21875 to 0.21875
- first_moment: float32 [16, 2048, 768], P('rep', 'lab'), may hold values from -6 to 6
- second_moment: float32 [16, 2048, 768], P('rep', 'lab'), may hold values from 0.5 to 8
Outputs:
- query_grad: float32 [65536, 768], P(('rep', 'lab'))
- new_weight: float32 [32768, 768], P('lab')
- new_first: float32 [16, 2048, 768], P('rep', 'lab')
- new_second: float32 [16, 2048, 768], P('rep', 'lab')
The draws below stay inside these ranges and needn't reach their ends.
Inputs may be any that keep to these rules, and one draw needn't show every extreme that they name: `shortlist`: the 8 blocks of one query are distinct; among the 128 rows of one device (aligned blocks of rows) no block is named by more than 8 rows, and some block is named by exactly 8.
All inputs are finite; a program needn't handle non-finite values.
Results may differ from the reference program's by a relative error of at most 0.0026.
Values may be sent and summed in bfloat16 or wider, within the bound.
No kernel may reach another device: no remote copies, remote signals or barrier semaphores. Data moves between devices by JAX's collectives and lax.ppermute only.
A program may use at most 64 MiB of HBM per device.

```python
import math
import jax
import jax.numpy as jnp
import numpy as np
from jax import lax

D = 768
BLOCK = 128
K = 8
CAP = 8
Q_DEV = 128
NBLK = 256
LABELS = 32768
QUERIES = 65536
SUB = 64
N_REP = 16
N_LAB = 32


def plant(values, own_key, low, top_value):
    dims = values.shape
    place = [jax.random.randint(jax.random.fold_in(own_key, axis), (), 0, dims[axis]) for axis in range(len(dims))]
    values = values.at[tuple(place)].set(low)
    longest = dims.index(max(dims))
    place[longest] = (place[longest] + 1) % dims[longest]
    return values.at[tuple(place)].set(top_value)


def level_of(rng, extent, shards, low, high):
    def one(dim, blocks):
        heights = jax.random.uniform(jax.random.fold_in(jax.random.fold_in(rng, 6), dim), (blocks,), jnp.float32, low / len(shards), high / len(shards))
        return jnp.repeat(jnp.exp(heights), extent[dim] // blocks).reshape((-1,) + (1,) * (len(extent) - dim - 1))

    factor_of = one(*shards[0])
    for cut in shards[1:]:
        factor_of = factor_of * one(*cut)
    return factor_of


def assign_block(rng, own, number, rows, count, top, limit, lean):
    ranking = jax.random.permutation(rng, count)
    packed, ordinary = shares(count, rows * top, limit, lean, True), shares(count, rows * top, limit, lean, False)
    places = jnp.arange(count)

    def named(lengths, offset_by):
        used = int((lengths > 0).sum())
        fixed = max(1, used // 4)
        passed = fixed + (places - fixed + offset_by * (used - fixed)) % max(1, count - fixed)
        return jnp.zeros((count,), jnp.int32).at[ranking[jnp.where(places < fixed, places, passed)]].set(jnp.asarray(lengths, jnp.int32))

    lengths = jnp.where(number % 4 == 0, named(packed, number // 4), named(ordinary, number - number // 4 - 1))
    mixed = jax.random.permutation(jax.random.fold_in(own, 3), count)
    giver, receiver = mixed[0:count // 2 * 2:2], mixed[1:count // 2 * 2:2]
    slack = jnp.minimum(lengths[giver] - 1, limit - lengths[receiver]) // 2
    slack = jnp.where((giver == ranking[0]) | (receiver == ranking[0]) | (lengths[receiver] == 0), 0, jnp.maximum(slack, 0))
    passed = jax.random.randint(jax.random.fold_in(own, 4), (count // 2,), 0, 1 << 20) % (slack + 1)
    lengths = lengths.at[giver].add(-passed).at[receiver].add(passed)
    items = jnp.searchsorted(jnp.cumsum(lengths), jnp.arange(rows * top), side="right").astype(jnp.int32)
    grid = items.reshape(top, rows).T
    grid = grid[jax.random.permutation(jax.random.fold_in(own, 1), rows)]
    offset_by = jax.random.randint(jax.random.fold_in(own, 2), (rows, 1), 0, top)
    return jnp.take_along_axis(grid, (jnp.arange(top)[None, :] + offset_by) % top, axis=1)


def shares(amount, total, bound, skew, full):
    portions = [(1 << 20) // math.isqrt(grade ** skew) + 1 for grade in range(1, amount + 1)]
    largest = bound if full else min(bound, max(-(-total // amount), total * portions[0] // sum(portions)))
    least = 1 if total - largest >= amount - 1 else 0
    given, rest = [largest] + [least] * (amount - 1), total - largest - least * (amount - 1)
    while rest > 0:
        candidates = [i for i in range(1, amount) if given[i] < largest] or [i for i in range(1, amount) if given[i] < bound]
        whole, budget = sum([portions[i] for i in candidates]), rest
        for i in candidates:
            more = min(bound - given[i], max(1, budget * portions[i] // whole), rest)
            given[i] = given[i] + more
            rest = rest - more
    return np.array(given)


def normal_values(stream_key, dims, deviation, limit, pieces=(), kind=jnp.bfloat16):
    factor_of = level_of(stream_key, dims, pieces, -0.22, 0.18) if pieces else 1.0
    values = jax.random.normal(stream_key, dims, jnp.float32) * deviation * factor_of
    return jnp.minimum(jnp.maximum(values, -limit), limit).astype(kind)


def setup_inputs(seed: int = 0) -> dict:
    streams_of = jax.random.split(jax.random.key(seed), 7)
    queries = normal_values(streams_of[0], (QUERIES, D), 1.0, 6.0, ((0, 512),))
    shortlist_keys = jax.random.split(jax.random.fold_in(streams_of[1], 1), QUERIES // Q_DEV)
    shortlist_turns = jax.random.permutation(jax.random.fold_in(streams_of[1], 3), QUERIES // Q_DEV)
    shortlist = jax.vmap(lambda own, number: assign_block(jax.random.fold_in(streams_of[1], 2), own, number, Q_DEV, NBLK, K, CAP, 2))(shortlist_keys, shortlist_turns).reshape((QUERIES, K))
    positive = plant(jax.random.randint(streams_of[2], (QUERIES, K), 0, 2 * BLOCK), jax.random.fold_in(streams_of[2], 1), 0, (2 * BLOCK) - 1).astype(jnp.int32)
    label_weight = normal_values(streams_of[3], (LABELS, D), D ** -0.5, 0.21875, ((0, 32),))
    first_moment = normal_values(streams_of[4], (N_REP, LABELS // N_REP, D), 1.0, 6.0, ((0, 16), (1, 32)), jnp.float32)
    second_moment = jnp.clip(jnp.exp(math.log(8.0) - 2.7725887 * jax.random.uniform(streams_of[5], (N_REP, LABELS // N_REP, D), jnp.float32) ** level_of(streams_of[5], (N_REP, LABELS // N_REP, D), ((0, 16), (1, 32)), -0.2, 0.2)), 0.5, 8.0)
    return dict(queries=queries, shortlist=shortlist, positive=positive, label_weight=label_weight, first_moment=first_moment, second_moment=second_moment)


beta_first = 0.9
beta_second = 0.999
learn_rate = 0.01
adam_epsilon = 1e-08
step_count = 100.0

def reference(queries, shortlist, positive, label_weight, first_moment, second_moment):
    blocks = label_weight.reshape(NBLK, BLOCK, D)
    offsets = jnp.arange(BLOCK, dtype=jnp.int32)
    width = min(64, QUERIES)

    def one_span(carry, inputs):
        rows, block_ids, targets = inputs
        label_tiles = blocks[block_ids].astype(jnp.float32)
        rows_wide = rows.astype(jnp.float32)
        logits = jnp.einsum('cd,ckld->ckl', rows_wide, label_tiles)
        labels = (offsets[None, None, :] == targets[:, :, None]).astype(jnp.float32)
        slopes = (jax.nn.sigmoid(logits) - labels).astype(jnp.bfloat16)
        slopes_wide = slopes.astype(jnp.float32)
        row_parts = jnp.einsum('ckl,ckld->ckd', slopes_wide, label_tiles)
        row_grad = lax.optimization_barrier(jnp.sum(row_parts, axis=1))
        weight_parts = jnp.einsum('ckl,cd->ckld', slopes_wide, rows_wide)
        carry = carry.at[block_ids.reshape(-1)].add(weight_parts.reshape(-1, BLOCK, D))
        return (carry, row_grad)
    start = jnp.zeros((NBLK, BLOCK, D), jnp.float32)
    inputs = (queries.reshape(-1, width, D), shortlist.reshape(-1, width, K), positive.reshape(-1, width, K))
    weight_grad, row_grads = lax.scan(one_span, start, inputs)
    query_grad = row_grads.reshape(QUERIES, D)
    grad_view = weight_grad.reshape(N_LAB, N_REP, SUB, D).transpose(1, 0, 2, 3).reshape(N_REP, LABELS // N_REP, D)
    new_first = beta_first * first_moment + (1.0 - beta_first) * grad_view
    new_second = beta_second * second_moment + (1.0 - beta_second) * grad_view * grad_view
    first_hat = new_first / (1.0 - beta_first ** step_count)
    second_hat = new_second / (1.0 - beta_second ** step_count)
    step_view = first_hat / (jnp.sqrt(second_hat) + adam_epsilon)
    step_rows = step_view.reshape(N_REP, N_LAB, SUB, D).transpose(1, 0, 2, 3).reshape(LABELS, D)
    new_weight = label_weight.astype(jnp.float32) - learn_rate * step_rows
    return (query_grad, new_weight, new_first, new_second)
```

```python
import functools

import jax
import jax.numpy as jnp
from jax import lax
from jax.experimental import pallas as pl
from jax.experimental.pallas import tpu as pltpu
from jax.sharding import PartitionSpec as P

D = 768
BLOCK = 128
K = 8
CAP = 8
LANES = 128
COLS = D // LANES
N_LAB = 32
N_Y = 8
BLK_DEV = 8
SLOTS = BLK_DEV * CAP
CHUNK = COLS * SLOTS
SUB = 64

beta_first = 0.9
beta_second = 0.999
learn_rate = 0.01
adam_epsilon = 1e-08
step_count = 100.0

bf16 = jnp.bfloat16
f32 = jnp.float32


def before_matrix():
    row = lax.broadcasted_iota(jnp.int32, (LANES, LANES), 0)
    col = lax.broadcasted_iota(jnp.int32, (LANES, LANES), 1)
    return (row < col).astype(f32).astype(bf16)


def slot_select(marks):
    named = marks >= 0.0
    earlier = jnp.dot(named.astype(f32).astype(bf16), before_matrix(), preferred_element_type=f32)
    rank = jnp.where(named, earlier, -1.0)
    slot = lax.broadcasted_iota(jnp.int32, (1, CAP, 1), 1).astype(f32)
    return rank[:, None, :] == slot


def send_kernel(short_ref, pos_ref, rows_ref, send_ref, pick_ref):
    nblk = N_LAB * BLK_DEV
    block = lax.broadcasted_iota(jnp.int32, (nblk, LANES), 0)
    marks = jnp.full((nblk, LANES), -1, jnp.int32)
    for k in range(K):
        marks = jnp.where(block == short_ref[k : k + 1, :], pos_ref[k : k + 1, :], marks)
    marks = marks.astype(f32)
    pick = slot_select(marks).astype(f32).reshape(nblk * CAP, LANES).astype(bf16)
    pick_ref[...] = pick
    send_ref[:, CHUNK : CHUNK + BLK_DEV, :] = marks.reshape(N_LAB, BLK_DEV, LANES).astype(bf16)
    rows = rows_ref[...]
    group = 4
    for g in range(N_LAB // group):
        chosen = jnp.dot(
            pick[g * group * SLOTS : (g + 1) * group * SLOTS], rows, preferred_element_type=f32
        ).astype(bf16)
        for o in range(group):
            for c in range(COLS):
                send_ref[g * group + o, c * SLOTS : (c + 1) * SLOTS, :] = chosen[
                    o * SLOTS : (o + 1) * SLOTS, c * LANES : (c + 1) * LANES
                ]


def pack_rows(short_t, pos_t, queries):
    return pl.pallas_call(
        send_kernel,
        out_shape=(
            jax.ShapeDtypeStruct((N_LAB, CHUNK + BLK_DEV, LANES), bf16),
            jax.ShapeDtypeStruct((N_LAB * SLOTS, LANES), bf16),
        ),
        cost_estimate=pl.CostEstimate(flops=400_000_000, bytes_accessed=4_000_000, transcendentals=0),
        name="pack_rows",
    )(short_t, pos_t, queries)


def block_kernel(where_ref, arrived_ref, tiles_ref, back_ref, keep_ref, give_ref, marks_ref, rows_ref):
    pair = pl.program_id(0)
    core = where_ref[1]

    @pl.when(pair == 0)
    def _():
        marks = arrived_ref[:, CHUNK : CHUNK + BLK_DEV, :].astype(f32)
        for b in range(BLK_DEV):
            marks_ref[b] = marks[:, b, :]

    for c in range(COLS):
        at = pl.ds(pl.multiple_of(c * SLOTS + pair * 2 * CAP, 2 * CAP), 2 * CAP)
        both = arrived_ref[:, at, :].astype(f32).reshape(N_LAB, 2, CAP, LANES)
        for h in range(2):
            rows_ref[h, :, c * LANES : (c + 1) * LANES] = (
                both[:, h].reshape(N_LAB * CAP, LANES).astype(bf16)
            )

    label = lax.broadcasted_iota(jnp.int32, (N_LAB * CAP, BLOCK), 1).astype(f32)
    parts = []
    for h in range(2):
        marks = marks_ref[pair * 2 + h]
        held = jnp.where(slot_select(marks), marks[:, None, :] + 1.0, 0.0)
        mark = (jnp.sum(held, axis=2, keepdims=True) - 1.0).reshape(N_LAB * CAP, 1)
        rows = rows_ref[h]
        tile = tiles_ref[h * BLOCK : (h + 1) * BLOCK, :]
        logits = lax.dot_general(rows, tile, (((1,), (1,)), ((), ())), preferred_element_type=f32)
        slopes = (jax.nn.sigmoid(logits) - (label == mark).astype(f32)).astype(bf16)
        parts.append(jnp.dot(slopes, tile, preferred_element_type=f32))
        grad = lax.dot_general(slopes, rows, (((0,), (0,)), ((), ())), preferred_element_type=f32)
        low, high = grad[:SUB], grad[SUB:]
        keep_ref[h] = jnp.where(core == 0, low, high)
        give_ref[h] = jnp.where(core == 0, high, low)
    for c in range(COLS):
        at = pl.ds(pl.multiple_of(c * SLOTS + pair * 2 * CAP, 2 * CAP), 2 * CAP)
        cols = slice(c * LANES, (c + 1) * LANES)
        both = jnp.stack([p[:, cols].reshape(N_LAB, CAP, LANES) for p in parts], axis=1)
        back_ref[:, at, :] = both.reshape(N_LAB, 2 * CAP, LANES).astype(bf16)


def label_blocks(where, arrived, label_weight):
    pairs = BLK_DEV // 2
    return pl.pallas_call(
        block_kernel,
        grid=(pairs,),
        in_specs=[
            pl.BlockSpec(memory_space=pltpu.SMEM),
            pl.BlockSpec((N_LAB, CHUNK + BLK_DEV, LANES), lambda p: (0, 0, 0)),
            pl.BlockSpec((2 * BLOCK, D), lambda p: (p, 0)),
        ],
        out_specs=[
            pl.BlockSpec((N_LAB, CHUNK, LANES), lambda p: (0, 0, 0)),
            pl.BlockSpec((2, SUB, D), lambda p: (p, 0, 0)),
            pl.BlockSpec((2, SUB, D), lambda p: (p, 0, 0)),
        ],
        out_shape=(
            jax.ShapeDtypeStruct((N_LAB, CHUNK, LANES), bf16),
            jax.ShapeDtypeStruct((BLK_DEV, SUB, D), f32),
            jax.ShapeDtypeStruct((BLK_DEV, SUB, D), f32),
        ),
        scratch_shapes=[
            pltpu.VMEM((BLK_DEV, N_LAB, LANES), f32),
            pltpu.VMEM((2, N_LAB * CAP, D), bf16),
        ],
        cost_estimate=pl.CostEstimate(
            flops=1_210_000_000, bytes_accessed=11_000_000, transcendentals=300_000
        ),
        name="label_blocks",
    )(where, arrived, label_weight)


def sum_kernel(pick_ref, back_ref, out_ref):
    step = pl.program_id(0)
    groups = back_ref.shape[0]
    pick = pick_ref[...]
    cols = []
    for c in range(COLS):
        part = back_ref[:, c * SLOTS : (c + 1) * SLOTS, :].reshape(groups * SLOTS, LANES)
        cols.append(part)
    parts = jnp.concatenate(cols, axis=1)
    total = lax.dot_general(pick, parts, (((0,), (0,)), ((), ())), preferred_element_type=f32)

    @pl.when(step == 0)
    def _():
        out_ref[...] = total

    @pl.when(step > 0)
    def _():
        out_ref[...] += total


def sum_parts(pick, back):
    steps = 4
    groups = N_LAB // steps
    return pl.pallas_call(
        sum_kernel,
        grid=(steps,),
        in_specs=[
            pl.BlockSpec((groups * SLOTS, LANES), lambda g: (g, 0)),
            pl.BlockSpec((groups, CHUNK, LANES), lambda g: (g, 0, 0)),
        ],
        out_specs=pl.BlockSpec((LANES, D), lambda g: (0, 0)),
        out_shape=jax.ShapeDtypeStruct((LANES, D), f32),
        cost_estimate=pl.CostEstimate(flops=400_000_000, bytes_accessed=4_000_000, transcendentals=0),
        name="sum_parts",
    )(pick, back)


def split_kernel(where_ref, keep_ref, got_ref, *out_refs):
    y = where_ref[0]
    for t in range(N_Y):
        to = lax.rem(y + t, N_Y)
        out_refs[t][...] = (keep_ref[to] + got_ref[to]).astype(out_refs[t].dtype)


def split_by_y(where, keep, got):
    return pl.pallas_call(
        split_kernel,
        in_specs=[
            pl.BlockSpec(memory_space=pltpu.SMEM),
            pl.BlockSpec(memory_space=pltpu.VMEM),
            pl.BlockSpec(memory_space=pltpu.VMEM),
        ],
        out_shape=tuple(
            jax.ShapeDtypeStruct((SUB, D), f32 if t == 0 else bf16) for t in range(N_Y)
        ),
        cost_estimate=pl.CostEstimate(flops=400_000, bytes_accessed=4_000_000, transcendentals=0),
        name="split_by_y",
    )(where, keep, got)


def weight_kernel(where_ref, tile_ref, mine_ref, other_ref, out_ref):
    core = where_ref[1]
    mine = mine_ref[0].astype(f32)
    other = other_ref[0].astype(f32)
    low = jnp.where(core == 0, mine, other)
    high = jnp.where(core == 0, other, mine)
    out_ref[:SUB, :] = tile_ref[:SUB, :].astype(f32) - learn_rate * low
    out_ref[SUB:, :] = tile_ref[SUB:, :].astype(f32) - learn_rate * high


def fresh_weight(where, label_weight, mine, other):
    def tile_at(t, where_ref):
        return (lax.rem(where_ref[0] - t + N_Y, N_Y), 0)

    def step_at(t, where_ref):
        return (t, 0, 0)

    return pl.pallas_call(
        weight_kernel,
        grid_spec=pltpu.PrefetchScalarGridSpec(
            num_scalar_prefetch=1,
            grid=(N_Y,),
            in_specs=[
                pl.BlockSpec((BLOCK, D), tile_at),
                pl.BlockSpec((1, SUB, D), step_at),
                pl.BlockSpec((1, SUB, D), step_at),
            ],
            out_specs=pl.BlockSpec((BLOCK, D), tile_at),
        ),
        out_shape=jax.ShapeDtypeStruct((N_Y * BLOCK, D), f32),
        cost_estimate=pl.CostEstimate(flops=1_600_000, bytes_accessed=6_300_000, transcendentals=0),
        name="fresh_weight",
    )(where, label_weight, mine, other)


def along_y(shift):
    return [(y * 2 + c, ((y + shift) % N_Y) * 2 + c) for y in range(N_Y) for c in range(2)]


OTHER_CORE = [(r, r ^ 1) for r in range(2 * N_Y)]


def body(queries, shortlist, positive, label_weight, first_moment, second_moment):
    rep = lax.axis_index("rep")
    where = jnp.stack([rep // 2, rep % 2]).astype(jnp.int32)
    send, pick = pack_rows(shortlist.T, positive.T, queries)
    arrived = lax.all_to_all(send, "lab", split_axis=0, concat_axis=0, tiled=True)
    back, keep, give = label_blocks(where, arrived, label_weight)
    returned = lax.all_to_all(back, "lab", split_axis=0, concat_axis=0, tiled=True)

    got = lax.ppermute(give, "rep", OTHER_CORE)
    shares = split_by_y(where, keep, got)
    grad = shares[0]
    for t in range(1, N_Y):
        grad = grad + lax.ppermute(shares[t], "rep", along_y(t)).astype(f32)
    grad = grad[None]
    new_first = beta_first * first_moment + (1.0 - beta_first) * grad
    new_second = beta_second * second_moment + (1.0 - beta_second) * grad * grad
    first_hat = new_first / (1.0 - beta_first**step_count)
    second_hat = new_second / (1.0 - beta_second**step_count)
    step = (first_hat / (jnp.sqrt(second_hat) + adam_epsilon)).astype(bf16)
    steps = [step] + [lax.ppermute(step, "rep", along_y(t)) for t in range(1, N_Y)]
    mine = jnp.concatenate(steps, axis=0)
    other = lax.ppermute(mine, "rep", OTHER_CORE)
    new_weight = fresh_weight(where, label_weight, mine, other)

    query_grad = sum_parts(pick, returned)
    return (query_grad, new_weight, new_first, new_second)


def solution(mesh):
    in_specs = (
        P(("rep", "lab"), None),
        P(("rep", "lab"), None),
        P(("rep", "lab"), None),
        P("lab", None),
        P("rep", "lab", None),
        P("rep", "lab", None),
    )
    out_specs = (
        P(("rep", "lab"), None),
        P("lab", None),
        P("rep", "lab", None),
        P("rep", "lab", None),
    )
    return jax.shard_map(body, mesh=mesh, in_specs=in_specs, out_specs=out_specs, check_vma=False)
```

```python
import functools

import jax
import jax.numpy as jnp
from jax import lax
from jax.experimental import pallas as pl
from jax.experimental.pallas import tpu as pltpu
from jax.sharding import PartitionSpec as P

D = 768
BLOCK = 128
K = 8
CAP = 8
LANES = 128
COLS = D // LANES
N_LAB = 32
N_Y = 8
BLK_DEV = 8
SLOTS = BLK_DEV * CAP
CHUNK = COLS * SLOTS
SUB = 64
FAR = N_Y // 2 - 1

beta_first = 0.9
beta_second = 0.999
learn_rate = 0.01
adam_epsilon = 1e-08
step_count = 100.0

bf16 = jnp.bfloat16
f32 = jnp.float32


def before_matrix():
    row = lax.broadcasted_iota(jnp.int32, (LANES, LANES), 0)
    col = lax.broadcasted_iota(jnp.int32, (LANES, LANES), 1)
    return (row < col).astype(f32).astype(bf16)


def slot_select(marks):
    named = marks >= 0.0
    earlier = jnp.dot(named.astype(f32).astype(bf16), before_matrix(), preferred_element_type=f32)
    rank = jnp.where(named, earlier, -1.0)
    slot = lax.broadcasted_iota(jnp.int32, (1, CAP, 1), 1).astype(f32)
    return rank[:, None, :] == slot


def send_kernel(short_ref, pos_ref, rows_ref, send_ref, pick_ref):
    nblk = N_LAB * BLK_DEV
    block = lax.broadcasted_iota(jnp.int32, (nblk, LANES), 0)
    marks = jnp.full((nblk, LANES), -1, jnp.int32)
    for k in range(K):
        marks = jnp.where(block == short_ref[k : k + 1, :], pos_ref[k : k + 1, :], marks)
    marks = marks.astype(f32)
    pick = slot_select(marks).astype(f32).reshape(nblk * CAP, LANES).astype(bf16)
    pick_ref[...] = pick
    send_ref[:, CHUNK : CHUNK + BLK_DEV, :] = marks.reshape(N_LAB, BLK_DEV, LANES).astype(bf16)
    rows = rows_ref[...]
    group = 4
    for g in range(N_LAB // group):
        chosen = jnp.dot(
            pick[g * group * SLOTS : (g + 1) * group * SLOTS], rows, preferred_element_type=f32
        ).astype(bf16)
        for o in range(group):
            for c in range(COLS):
                send_ref[g * group + o, c * SLOTS : (c + 1) * SLOTS, :] = chosen[
                    o * SLOTS : (o + 1) * SLOTS, c * LANES : (c + 1) * LANES
                ]


def pack_rows(short_t, pos_t, queries):
    return pl.pallas_call(
        send_kernel,
        out_shape=(
            jax.ShapeDtypeStruct((N_LAB, CHUNK + BLK_DEV, LANES), bf16),
            jax.ShapeDtypeStruct((N_LAB * SLOTS, LANES), bf16),
        ),
        cost_estimate=pl.CostEstimate(flops=400_000_000, bytes_accessed=4_000_000, transcendentals=0),
        name="pack_rows",
    )(short_t, pos_t, queries)


def block_kernel(where_ref, arrived_ref, tiles_ref, back_ref, keep_ref, give_ref, marks_ref, rows_ref):
    pair = pl.program_id(0)
    y, core = where_ref[0], where_ref[1]

    @pl.when(pair == 0)
    def _():
        marks = arrived_ref[:, CHUNK : CHUNK + BLK_DEV, :].astype(f32)
        for b in range(BLK_DEV):
            marks_ref[b] = marks[:, b, :]

    for c in range(COLS):
        at = pl.ds(pl.multiple_of(c * SLOTS + pair * 2 * CAP, 2 * CAP), 2 * CAP)
        both = arrived_ref[:, at, :].astype(f32).reshape(N_LAB, 2, CAP, LANES)
        for h in range(2):
            rows_ref[h, :, c * LANES : (c + 1) * LANES] = (
                both[:, h].reshape(N_LAB * CAP, LANES).astype(bf16)
            )

    label = lax.broadcasted_iota(jnp.int32, (N_LAB * CAP, BLOCK), 1).astype(f32)
    parts = []
    for h in range(2):
        marks = marks_ref[pair * 2 + h]
        held = jnp.where(slot_select(marks), marks[:, None, :] + 1.0, 0.0)
        mark = (jnp.sum(held, axis=2, keepdims=True) - 1.0).reshape(N_LAB * CAP, 1)
        rows = rows_ref[h]
        tile = tiles_ref[h * BLOCK : (h + 1) * BLOCK, :]
        logits = lax.dot_general(rows, tile, (((1,), (1,)), ((), ())), preferred_element_type=f32)
        slopes = (jax.nn.sigmoid(logits) - (label == mark).astype(f32)).astype(bf16)
        parts.append(jnp.dot(slopes, tile, preferred_element_type=f32))
        grad = lax.dot_general(slopes, rows, (((0,), (0,)), ((), ())), preferred_element_type=f32)
        ahead = lax.rem(pair * 2 + h - y + N_Y, N_Y)
        halved = lax.rem(ahead, N_Y // 2) == 0
        first = ahead < N_Y // 2
        unit = jnp.where(first, ahead, N_Y - ahead) * 2 - 2
        own = jnp.where(first, 0, 1) == core
        for i in range(2):
            at = jnp.where(halved, jnp.where(first, N_Y - 1, N_Y - 2), unit + i)
            kept = jnp.where(halved, core == i, own)

            @pl.when(kept)
            def _():
                keep_ref[at] = grad[i * SUB : (i + 1) * SUB]

            @pl.when(jnp.logical_not(kept))
            def _():
                give_ref[at] = grad[i * SUB : (i + 1) * SUB]

    for c in range(COLS):
        at = pl.ds(pl.multiple_of(c * SLOTS + pair * 2 * CAP, 2 * CAP), 2 * CAP)
        cols = slice(c * LANES, (c + 1) * LANES)
        both = jnp.stack([p[:, cols].reshape(N_LAB, CAP, LANES) for p in parts], axis=1)
        back_ref[:, at, :] = both.reshape(N_LAB, 2 * CAP, LANES).astype(bf16)


def label_blocks(where, arrived, label_weight):
    pairs = BLK_DEV // 2
    return pl.pallas_call(
        block_kernel,
        grid=(pairs,),
        in_specs=[
            pl.BlockSpec(memory_space=pltpu.SMEM),
            pl.BlockSpec((N_LAB, CHUNK + BLK_DEV, LANES), lambda p: (0, 0, 0)),
            pl.BlockSpec((2 * BLOCK, D), lambda p: (p, 0)),
        ],
        out_specs=[
            pl.BlockSpec((N_LAB, CHUNK, LANES), lambda p: (0, 0, 0)),
            pl.BlockSpec((N_Y, SUB, D), lambda p: (0, 0, 0)),
            pl.BlockSpec((N_Y, SUB, D), lambda p: (0, 0, 0)),
        ],
        out_shape=(
            jax.ShapeDtypeStruct((N_LAB, CHUNK, LANES), bf16),
            jax.ShapeDtypeStruct((BLK_DEV, SUB, D), f32),
            jax.ShapeDtypeStruct((BLK_DEV, SUB, D), f32),
        ),
        scratch_shapes=[
            pltpu.VMEM((BLK_DEV, N_LAB, LANES), f32),
            pltpu.VMEM((2, N_LAB * CAP, D), bf16),
        ],
        cost_estimate=pl.CostEstimate(
            flops=1_210_000_000, bytes_accessed=11_000_000, transcendentals=300_000
        ),
        name="label_blocks",
    )(where, arrived, label_weight)


def sum_kernel(pick_ref, back_ref, out_ref):
    step = pl.program_id(0)
    groups = back_ref.shape[0]
    pick = pick_ref[...]
    cols = []
    for c in range(COLS):
        part = back_ref[:, c * SLOTS : (c + 1) * SLOTS, :].reshape(groups * SLOTS, LANES)
        cols.append(part)
    parts = jnp.concatenate(cols, axis=1)
    total = lax.dot_general(pick, parts, (((0,), (0,)), ((), ())), preferred_element_type=f32)

    @pl.when(step == 0)
    def _():
        out_ref[...] = total

    @pl.when(step > 0)
    def _():
        out_ref[...] += total


def sum_parts(pick, back):
    steps = 4
    groups = N_LAB // steps
    return pl.pallas_call(
        sum_kernel,
        grid=(steps,),
        in_specs=[
            pl.BlockSpec((groups * SLOTS, LANES), lambda g: (g, 0)),
            pl.BlockSpec((groups, CHUNK, LANES), lambda g: (g, 0, 0)),
        ],
        out_specs=pl.BlockSpec((LANES, D), lambda g: (0, 0)),
        out_shape=jax.ShapeDtypeStruct((LANES, D), f32),
        cost_estimate=pl.CostEstimate(flops=400_000_000, bytes_accessed=4_000_000, transcendentals=0),
        name="sum_parts",
    )(pick, back)


def split_kernel(keep_ref, got_ref, *out_refs):
    for s in range(FAR):
        for i in range(2):
            u = 2 * s + i
            out_refs[s][i * SUB : (i + 1) * SUB, :] = (keep_ref[u] + got_ref[u]).astype(bf16)
    out_refs[FAR][...] = (keep_ref[2 * FAR] + got_ref[2 * FAR]).astype(bf16)
    out_refs[FAR + 1][...] = keep_ref[2 * FAR + 1] + got_ref[2 * FAR + 1]


def split_by_y(keep, got):
    return pl.pallas_call(
        split_kernel,
        out_shape=tuple(jax.ShapeDtypeStruct((BLOCK, D), bf16) for _ in range(FAR))
        + (jax.ShapeDtypeStruct((SUB, D), bf16), jax.ShapeDtypeStruct((SUB, D), f32)),
        cost_estimate=pl.CostEstimate(flops=400_000, bytes_accessed=4_000_000, transcendentals=0),
        name="split_by_y",
    )(keep, got)


def weight_block(tile_ref, out_ref, step):
    out_ref[...] = tile_ref[...].astype(f32) - learn_rate * step.astype(f32)


def near_kernel(where_ref, tile_ref, both_ref, one_ref, two_ref, three_ref, out_ref):
    step = pl.program_id(0)
    for i, ref in enumerate((both_ref, one_ref, two_ref, three_ref)):

        @pl.when(step == i)
        def _():
            weight_block(tile_ref, out_ref, ref[...])


def far_kernel(where_ref, tile_ref, mine_ref, other_ref, begun_ref, out_ref):
    step = pl.program_id(0)
    core = where_ref[1]

    @pl.when(step == 0)
    def _():
        mine = mine_ref[...].astype(f32)
        other = other_ref[FAR * BLOCK :, :].astype(f32)
        low = jnp.where(core == 0, mine, other)
        high = jnp.where(core == 0, other, mine)
        weight_block(tile_ref, out_ref, jnp.concatenate([low, high], axis=0))

    for i in range(FAR):

        @pl.when(step == i + 1)
        def _():
            weight_block(tile_ref, out_ref, other_ref[i * BLOCK : (i + 1) * BLOCK, :])


def way(where_ref):
    return 1 - 2 * where_ref[1]


def near_tile(t, where_ref):
    return (lax.rem(where_ref[0] - way(where_ref) * t + N_Y, N_Y), 0)


def far_tile(t, where_ref):
    ahead = jnp.where(t == 0, N_Y // 2, way(where_ref) * t)
    return (lax.rem(where_ref[0] + ahead + N_Y, N_Y), 0)


def whole(shape):
    return pl.BlockSpec(shape, lambda t, where_ref: (0,) * len(shape))


def fresh_weight(where, label_weight, both, near, opposite, other):
    out_shape = jax.ShapeDtypeStruct((N_Y * BLOCK, D), f32)
    cost = pl.CostEstimate(flops=800_000, bytes_accessed=3_200_000, transcendentals=0)
    begun = pl.pallas_call(
        near_kernel,
        grid_spec=pltpu.PrefetchScalarGridSpec(
            num_scalar_prefetch=1,
            grid=(N_Y // 2,),
            in_specs=[pl.BlockSpec((BLOCK, D), near_tile)] + [whole((BLOCK, D))] * 4,
            out_specs=pl.BlockSpec((BLOCK, D), near_tile),
        ),
        out_shape=out_shape,
        cost_estimate=cost,
        name="near_weight",
    )(where, label_weight, both, *near)
    return pl.pallas_call(
        far_kernel,
        grid_spec=pltpu.PrefetchScalarGridSpec(
            num_scalar_prefetch=1,
            grid=(N_Y // 2,),
            in_specs=[
                pl.BlockSpec((BLOCK, D), far_tile),
                whole((SUB, D)),
                whole((FAR * BLOCK + SUB, D)),
                pl.BlockSpec(memory_space=pl.ANY),
            ],
            out_specs=pl.BlockSpec((BLOCK, D), far_tile),
        ),
        out_shape=out_shape,
        input_output_aliases={4: 0},
        cost_estimate=cost,
        name="far_weight",
    )(where, label_weight, opposite, other, begun)


def along_y(shift):
    return [(y * 2 + c, ((y + (1 - 2 * c) * shift) % N_Y) * 2 + c) for y in range(N_Y) for c in range(2)]


OTHER_CORE = [(r, r ^ 1) for r in range(2 * N_Y)]


def body(queries, shortlist, positive, label_weight, first_moment, second_moment):
    rep = lax.axis_index("rep")
    where = jnp.stack([rep // 2, rep % 2]).astype(jnp.int32)
    send, pick = pack_rows(shortlist.T, positive.T, queries)
    arrived = lax.all_to_all(send, "lab", split_axis=0, concat_axis=0, tiled=True)
    back, keep, give = label_blocks(where, arrived, label_weight)
    returned = lax.all_to_all(back, "lab", split_axis=0, concat_axis=0, tiled=True)

    got = lax.ppermute(give, "rep", OTHER_CORE)
    *sides, opposite, grad = split_by_y(keep, got)
    side = jnp.zeros((BLOCK, D), f32)
    for i, share in enumerate(sides):
        side = side + lax.ppermute(share, "rep", along_y(i + 1)).astype(f32)
    grad = grad + lax.ppermute(opposite, "rep", along_y(N_Y // 2)).astype(f32)
    low, high = side[:SUB], side[SUB:]
    first_core = where[1] == 0
    grad = grad + jnp.where(first_core, low, high)
    grad = grad + lax.ppermute(jnp.where(first_core, high, low), "rep", OTHER_CORE)
    grad = grad[None]
    new_first = beta_first * first_moment + (1.0 - beta_first) * grad
    new_second = beta_second * second_moment + (1.0 - beta_second) * grad * grad
    first_hat = new_first / (1.0 - beta_first**step_count)
    second_hat = new_second / (1.0 - beta_second**step_count)
    step = (first_hat / (jnp.sqrt(second_hat) + adam_epsilon)).astype(bf16)[0]
    opposite = lax.ppermute(step, "rep", along_y(N_Y // 2))
    theirs = lax.ppermute(step, "rep", OTHER_CORE)
    both = jnp.concatenate(
        [jnp.where(first_core, step, theirs), jnp.where(first_core, theirs, step)], axis=0
    )
    near = [lax.ppermute(both, "rep", along_y(i + 1)) for i in range(FAR)]
    other = lax.ppermute(jnp.concatenate([*near, opposite], axis=0), "rep", OTHER_CORE)
    new_weight = fresh_weight(where, label_weight, both, near, opposite, other)

    query_grad = sum_parts(pick, returned)
    return (query_grad, new_weight, new_first, new_second)


def solution(mesh):
    in_specs = (
        P(("rep", "lab"), None),
        P(("rep", "lab"), None),
        P(("rep", "lab"), None),
        P("lab", None),
        P("rep", "lab", None),
        P("rep", "lab", None),
    )
    out_specs = (
        P(("rep", "lab"), None),
        P("lab", None),
        P("rep", "lab", None),
        P("rep", "lab", None),
    )
    return jax.shard_map(body, mesh=mesh, in_specs=in_specs, out_specs=out_specs, check_vma=False)
```

```python
import jax
import jax.numpy as jnp
from jax import lax
from jax.experimental import pallas as pl
from jax.experimental.pallas import tpu as pltpu
from jax.sharding import Mesh
from jax.sharding import PartitionSpec as P

D = 768
BLOCK = 128
K = 8
CAP = 8
LANES = 128
COLS = D // LANES
N_LAB = 32
N_X = 4
N_Z = 8
Q_DEV = 128
UP = 4
ACROSS = COLS - UP
N_Y = 8
BLK_DEV = 8
SLOTS = BLK_DEV * CAP
CHUNK = COLS * SLOTS
SUB = 64
FAR = N_Y // 2 - 1

beta_first = 0.9
beta_second = 0.999
learn_rate = 0.01
adam_epsilon = 1e-08
step_count = 100.0

bf16 = jnp.bfloat16
f32 = jnp.float32


def before_matrix():
    row = lax.broadcasted_iota(jnp.int32, (LANES, LANES), 0)
    col = lax.broadcasted_iota(jnp.int32, (LANES, LANES), 1)
    return (row < col).astype(f32).astype(bf16)


def slot_select(marks):
    named = marks >= 0.0
    earlier = jnp.dot(named.astype(f32).astype(bf16), before_matrix(), preferred_element_type=f32)
    rank = jnp.where(named, earlier, -1.0)
    slot = lax.broadcasted_iota(jnp.int32, (1, CAP, 1), 1).astype(f32)
    return rank[:, None, :] == slot


def begin_kernel(short_ref, pos_ref, rows_ref, up_ref, across_ref):
    info = jnp.concatenate([short_ref[...], pos_ref[...]], axis=0).astype(f32).astype(bf16)
    for c in range(COLS):
        part = rows_ref[:, c * LANES : (c + 1) * LANES]
        if c < UP:
            for z in range(N_Z):
                up_ref[z, c * Q_DEV : (c + 1) * Q_DEV, :] = part
        else:
            across_ref[(c - UP) * Q_DEV : (c - UP + 1) * Q_DEV, :] = part
    for z in range(N_Z):
        up_ref[z, UP * Q_DEV :, :] = info
    across_ref[ACROSS * Q_DEV :, :] = info


def begin(short_t, pos_t, queries):
    return pl.pallas_call(
        begin_kernel,
        out_shape=(
            jax.ShapeDtypeStruct((N_Z, UP * Q_DEV + 2 * K, LANES), bf16),
            jax.ShapeDtypeStruct((ACROSS * Q_DEV + 2 * K, LANES), bf16),
        ),
        cost_estimate=pl.CostEstimate(flops=0, bytes_accessed=1_500_000, transcendentals=0),
        name="begin",
    )(short_t, pos_t, queries)


def marks_of(block, short, positive):
    marks = jnp.full(block.shape, -1.0, f32)
    for k in range(K):
        marks = jnp.where(block == short[k : k + 1, :], positive[k : k + 1, :], marks)
    return marks


def one_hot(marks):
    return slot_select(marks).astype(f32).reshape(marks.shape[0] * CAP, LANES).astype(bf16)


def across_kernel(where_ref, short_ref, pos_ref, *refs):
    *source_refs, out_ref, pick_ref = refs
    x = where_ref[2]
    nblk = N_LAB * BLK_DEV
    every = lax.broadcasted_iota(jnp.int32, (nblk, LANES), 0).astype(f32)
    short, positive = short_ref[...].astype(f32), pos_ref[...].astype(f32)
    pick_ref[...] = one_hot(marks_of(every, short, positive))
    here = N_Z * BLK_DEV
    block = (lax.broadcasted_iota(jnp.int32, (here, LANES), 0) + x * here).astype(f32)
    marks = []
    for ref in source_refs:
        info = ref[ACROSS * Q_DEV :, :].astype(f32)
        marks.append(marks_of(block, info[:K], info[K:]))
    pick = one_hot(jnp.concatenate(marks, axis=0))
    for t, ref in enumerate(source_refs):
        rows = jnp.concatenate(
            [ref[c * Q_DEV : (c + 1) * Q_DEV, :] for c in range(ACROSS)], axis=1
        )
        chosen = jnp.dot(
            pick[t * here * CAP : (t + 1) * here * CAP], rows, preferred_element_type=f32
        ).astype(bf16)
        for z in range(N_Z):
            for c in range(ACROSS):
                out_ref[z, t, c * SLOTS : (c + 1) * SLOTS, :] = chosen[
                    z * SLOTS : (z + 1) * SLOTS, c * LANES : (c + 1) * LANES
                ]


def select_across(where, short_t, pos_t, sources):
    return pl.pallas_call(
        across_kernel,
        in_specs=[pl.BlockSpec(memory_space=pltpu.SMEM)]
        + [pl.BlockSpec(memory_space=pltpu.VMEM)] * (2 + N_X),
        out_shape=(
            jax.ShapeDtypeStruct((N_Z, N_X, ACROSS * SLOTS, LANES), bf16),
            jax.ShapeDtypeStruct((N_LAB * SLOTS, LANES), bf16),
        ),
        cost_estimate=pl.CostEstimate(flops=200_000_000, bytes_accessed=2_000_000, transcendentals=0),
        name="select_across",
    )(where, short_t, pos_t, *sources)


def up_kernel(where_ref, arrived_ref, *out_refs):
    x, z = where_ref[2], where_ref[3]
    index = lax.broadcasted_iota(jnp.int32, (N_X * BLK_DEV, LANES), 0)
    owner_x = (index // BLK_DEV + x) % N_X
    block = (owner_x * (N_Z * BLK_DEV) + z * BLK_DEV + index % BLK_DEV).astype(f32)
    marks = []
    for s in range(N_Z):
        info = arrived_ref[s, UP * Q_DEV :, :].astype(f32)
        marks.append(marks_of(block, info[:K], info[K:]))
    pick = one_hot(jnp.concatenate(marks, axis=0))
    count = N_X * SLOTS
    for s in range(N_Z):
        rows = jnp.concatenate(
            [arrived_ref[s, c * Q_DEV : (c + 1) * Q_DEV, :] for c in range(UP)], axis=1
        )
        chosen = jnp.dot(
            pick[s * count : (s + 1) * count], rows, preferred_element_type=f32
        ).astype(bf16)
        for t in range(N_X):
            for c in range(UP):
                out_refs[t][s, c * SLOTS : (c + 1) * SLOTS, :] = chosen[
                    t * SLOTS : (t + 1) * SLOTS, c * LANES : (c + 1) * LANES
                ]
            out_refs[t][s, UP * SLOTS :, :] = marks[s][t * BLK_DEV : (t + 1) * BLK_DEV].astype(bf16)


def select_up(where, arrived):
    return pl.pallas_call(
        up_kernel,
        in_specs=[
            pl.BlockSpec(memory_space=pltpu.SMEM),
            pl.BlockSpec(memory_space=pltpu.VMEM),
        ],
        out_shape=tuple(
            jax.ShapeDtypeStruct((N_Z, UP * SLOTS + BLK_DEV, LANES), bf16) for _ in range(N_X)
        ),
        cost_estimate=pl.CostEstimate(flops=300_000_000, bytes_accessed=3_000_000, transcendentals=0),
        name="select_up",
    )(where, arrived)


def block_kernel(
    where_ref, a0_ref, a1_ref, a2_ref, a3_ref, b_ref, tiles_ref, back_ref, keep_ref, give_ref, marks_ref, rows_ref
):
    a_refs = (a0_ref, a1_ref, a2_ref, a3_ref)
    x = where_ref[2]
    pair = pl.program_id(0)
    y, core = where_ref[0], where_ref[1]

    @pl.when(pair == 0)
    def _():
        for t in range(N_X):
            marks = a_refs[t][:, UP * SLOTS :, :].astype(f32)
            for b in range(BLK_DEV):
                marks_ref[b, t * N_Z : (t + 1) * N_Z, :] = marks[:, b, :]

    for c in range(COLS):
        group = c if c < UP else c - UP
        at = pl.ds(pl.multiple_of(group * SLOTS + pair * 2 * CAP, 2 * CAP), 2 * CAP)
        for t in range(N_X):
            part = a_refs[t][:, at, :] if c < UP else b_ref[:, t, at, :]
            both = part.astype(f32).reshape(N_Z, 2, CAP, LANES)
            for h in range(2):
                rows_ref[h, t * SLOTS : (t + 1) * SLOTS, c * LANES : (c + 1) * LANES] = (
                    both[:, h].reshape(N_Z * CAP, LANES).astype(bf16)
                )

    label = lax.broadcasted_iota(jnp.int32, (N_LAB * CAP, BLOCK), 1).astype(f32)
    parts = []
    for h in range(2):
        marks = marks_ref[pair * 2 + h]
        held = jnp.where(slot_select(marks), marks[:, None, :] + 1.0, 0.0)
        mark = (jnp.sum(held, axis=2, keepdims=True) - 1.0).reshape(N_LAB * CAP, 1)
        rows = rows_ref[h]
        tile = tiles_ref[h * BLOCK : (h + 1) * BLOCK, :]
        logits = lax.dot_general(rows, tile, (((1,), (1,)), ((), ())), preferred_element_type=f32)
        slopes = (jax.nn.sigmoid(logits) - (label == mark).astype(f32)).astype(bf16)
        parts.append(jnp.dot(slopes, tile, preferred_element_type=f32))
        grad = lax.dot_general(slopes, rows, (((0,), (0,)), ((), ())), preferred_element_type=f32)
        ahead = lax.rem(pair * 2 + h - y + N_Y, N_Y)
        halved = lax.rem(ahead, N_Y // 2) == 0
        first = ahead < N_Y // 2
        unit = jnp.where(first, ahead, N_Y - ahead) * 2 - 2
        own = jnp.where(first, 0, 1) == core
        for i in range(2):
            at = jnp.where(halved, jnp.where(first, N_Y - 1, N_Y - 2), unit + i)
            kept = jnp.where(halved, core == i, own)

            @pl.when(kept)
            def _():
                keep_ref[at] = grad[i * SUB : (i + 1) * SUB]

            @pl.when(jnp.logical_not(kept))
            def _():
                give_ref[at] = grad[i * SUB : (i + 1) * SUB]

    for c in range(COLS):
        at = pl.ds(pl.multiple_of(c * SLOTS + pair * 2 * CAP, 2 * CAP), 2 * CAP)
        cols = slice(c * LANES, (c + 1) * LANES)
        both = jnp.stack([p[:, cols].reshape(N_LAB, CAP, LANES) for p in parts], axis=1)
        both = both.reshape(N_LAB, 2 * CAP, LANES).astype(bf16)
        for t in range(N_X):
            source_x = lax.rem(x - t + N_X, N_X)
            back_ref[pl.ds(source_x * N_Z, N_Z), at, :] = both[t * N_Z : (t + 1) * N_Z]


def label_blocks(where, up, across, label_weight):
    pairs = BLK_DEV // 2
    return pl.pallas_call(
        block_kernel,
        grid=(pairs,),
        in_specs=[
            pl.BlockSpec(memory_space=pltpu.SMEM),
        ]
        + [pl.BlockSpec((N_Z, UP * SLOTS + BLK_DEV, LANES), lambda p: (0, 0, 0))] * N_X
        + [
            pl.BlockSpec((N_Z, N_X, ACROSS * SLOTS, LANES), lambda p: (0, 0, 0, 0)),
            pl.BlockSpec((2 * BLOCK, D), lambda p: (p, 0)),
        ],
        out_specs=[
            pl.BlockSpec((N_LAB, CHUNK, LANES), lambda p: (0, 0, 0)),
            pl.BlockSpec((N_Y, SUB, D), lambda p: (0, 0, 0)),
            pl.BlockSpec((N_Y, SUB, D), lambda p: (0, 0, 0)),
        ],
        out_shape=(
            jax.ShapeDtypeStruct((N_LAB, CHUNK, LANES), bf16),
            jax.ShapeDtypeStruct((BLK_DEV, SUB, D), f32),
            jax.ShapeDtypeStruct((BLK_DEV, SUB, D), f32),
        ),
        scratch_shapes=[
            pltpu.VMEM((BLK_DEV, N_LAB, LANES), f32),
            pltpu.VMEM((2, N_LAB * CAP, D), bf16),
        ],
        cost_estimate=pl.CostEstimate(
            flops=1_210_000_000, bytes_accessed=11_000_000, transcendentals=300_000
        ),
        name="label_blocks",
    )(where, *up, across, label_weight)


def sum_kernel(pick_ref, back_ref, out_ref):
    step = pl.program_id(0)
    groups = back_ref.shape[0]
    pick = pick_ref[...]
    cols = []
    for c in range(COLS):
        part = back_ref[:, c * SLOTS : (c + 1) * SLOTS, :].reshape(groups * SLOTS, LANES)
        cols.append(part)
    parts = jnp.concatenate(cols, axis=1)
    total = lax.dot_general(pick, parts, (((0,), (0,)), ((), ())), preferred_element_type=f32)

    @pl.when(step == 0)
    def _():
        out_ref[...] = total

    @pl.when(step > 0)
    def _():
        out_ref[...] += total


def sum_parts(pick, back):
    steps = 4
    groups = N_LAB // steps
    return pl.pallas_call(
        sum_kernel,
        grid=(steps,),
        in_specs=[
            pl.BlockSpec((groups * SLOTS, LANES), lambda g: (g, 0)),
            pl.BlockSpec((groups, CHUNK, LANES), lambda g: (g, 0, 0)),
        ],
        out_specs=pl.BlockSpec((LANES, D), lambda g: (0, 0)),
        out_shape=jax.ShapeDtypeStruct((LANES, D), f32),
        cost_estimate=pl.CostEstimate(flops=400_000_000, bytes_accessed=4_000_000, transcendentals=0),
        name="sum_parts",
    )(pick, back)


def split_kernel(keep_ref, got_ref, *out_refs):
    for s in range(FAR):
        for i in range(2):
            u = 2 * s + i
            out_refs[s][i * SUB : (i + 1) * SUB, :] = (keep_ref[u] + got_ref[u]).astype(bf16)
    out_refs[FAR][...] = (keep_ref[2 * FAR] + got_ref[2 * FAR]).astype(bf16)
    out_refs[FAR + 1][...] = keep_ref[2 * FAR + 1] + got_ref[2 * FAR + 1]


def split_by_y(keep, got):
    return pl.pallas_call(
        split_kernel,
        out_shape=tuple(jax.ShapeDtypeStruct((BLOCK, D), bf16) for _ in range(FAR))
        + (jax.ShapeDtypeStruct((SUB, D), bf16), jax.ShapeDtypeStruct((SUB, D), f32)),
        cost_estimate=pl.CostEstimate(flops=400_000, bytes_accessed=4_000_000, transcendentals=0),
        name="split_by_y",
    )(keep, got)


def weight_block(tile_ref, out_ref, step):
    out_ref[...] = tile_ref[...].astype(f32) - learn_rate * step.astype(f32)


def near_kernel(where_ref, tile_ref, both_ref, one_ref, two_ref, three_ref, out_ref):
    step = pl.program_id(0)
    for i, ref in enumerate((both_ref, one_ref, two_ref, three_ref)):

        @pl.when(step == i)
        def _():
            weight_block(tile_ref, out_ref, ref[...])


def far_kernel(where_ref, tile_ref, mine_ref, other_ref, begun_ref, out_ref):
    step = pl.program_id(0)
    core = where_ref[1]

    @pl.when(step == 0)
    def _():
        mine = mine_ref[...].astype(f32)
        other = other_ref[FAR * BLOCK :, :].astype(f32)
        low = jnp.where(core == 0, mine, other)
        high = jnp.where(core == 0, other, mine)
        weight_block(tile_ref, out_ref, jnp.concatenate([low, high], axis=0))

    for i in range(FAR):

        @pl.when(step == i + 1)
        def _():
            weight_block(tile_ref, out_ref, other_ref[i * BLOCK : (i + 1) * BLOCK, :])


def way(where_ref):
    return 1 - 2 * where_ref[1]


def near_tile(t, where_ref):
    return (lax.rem(where_ref[0] - way(where_ref) * t + N_Y, N_Y), 0)


def far_tile(t, where_ref):
    ahead = jnp.where(t == 0, N_Y // 2, way(where_ref) * t)
    return (lax.rem(where_ref[0] + ahead + N_Y, N_Y), 0)


def whole(shape):
    return pl.BlockSpec(shape, lambda t, where_ref: (0,) * len(shape))


def fresh_weight(where, label_weight, both, near, opposite, other):
    out_shape = jax.ShapeDtypeStruct((N_Y * BLOCK, D), f32)
    cost = pl.CostEstimate(flops=800_000, bytes_accessed=3_200_000, transcendentals=0)
    begun = pl.pallas_call(
        near_kernel,
        grid_spec=pltpu.PrefetchScalarGridSpec(
            num_scalar_prefetch=1,
            grid=(N_Y // 2,),
            in_specs=[pl.BlockSpec((BLOCK, D), near_tile)] + [whole((BLOCK, D))] * 4,
            out_specs=pl.BlockSpec((BLOCK, D), near_tile),
        ),
        out_shape=out_shape,
        cost_estimate=cost,
        name="near_weight",
    )(where, label_weight, both, *near)
    return pl.pallas_call(
        far_kernel,
        grid_spec=pltpu.PrefetchScalarGridSpec(
            num_scalar_prefetch=1,
            grid=(N_Y // 2,),
            in_specs=[
                pl.BlockSpec((BLOCK, D), far_tile),
                whole((SUB, D)),
                whole((FAR * BLOCK + SUB, D)),
                pl.BlockSpec(memory_space=pl.ANY),
            ],
            out_specs=pl.BlockSpec((BLOCK, D), far_tile),
        ),
        out_shape=out_shape,
        input_output_aliases={4: 0},
        cost_estimate=cost,
        name="far_weight",
    )(where, label_weight, opposite, other, begun)


def along_y(shift):
    return [(y * 2 + c, ((y + (1 - 2 * c) * shift) % N_Y) * 2 + c) for y in range(N_Y) for c in range(2)]


OTHER_CORE = [(r, r ^ 1) for r in range(2 * N_Y)]


def along_x(shift):
    return [(x, (x + shift) % N_X) for x in range(N_X)]


def body(queries, shortlist, positive, label_weight, first_moment, second_moment):
    rep = lax.axis_index("rep")
    where = jnp.stack([rep // 2, rep % 2, lax.axis_index("x"), lax.axis_index("z")])
    where = where.astype(jnp.int32)
    short_t, pos_t = shortlist.T, positive.T
    up, across = begin(short_t, pos_t, queries)
    up = lax.all_to_all(up, "z", split_axis=0, concat_axis=0, tiled=True)
    sources = [across] + [lax.ppermute(across, "x", along_x(t)) for t in range(1, N_X)]
    across, pick = select_across(where, short_t, pos_t, sources)
    across = lax.all_to_all(across, "z", split_axis=0, concat_axis=0, tiled=True)
    up = select_up(where, up)
    up = [up[0]] + [lax.ppermute(up[t], "x", along_x(t)) for t in range(1, N_X)]
    back, keep, give = label_blocks(where, up, across, label_weight)
    returned = lax.all_to_all(back, ("x", "z"), split_axis=0, concat_axis=0, tiled=True)

    got = lax.ppermute(give, "rep", OTHER_CORE)
    *sides, opposite, grad = split_by_y(keep, got)
    side = jnp.zeros((BLOCK, D), f32)
    for i, share in enumerate(sides):
        side = side + lax.ppermute(share, "rep", along_y(i + 1)).astype(f32)
    first_core = where[1] == 0
    far = lax.ppermute(opposite, "rep", along_y(N_Y // 2)).astype(f32)
    low = side[:SUB] + jnp.where(first_core, far, 0.0)
    high = side[SUB:] + jnp.where(first_core, 0.0, far)
    grad = grad + jnp.where(first_core, low, high)
    grad = grad + lax.ppermute(jnp.where(first_core, high, low), "rep", OTHER_CORE)
    grad = grad[None]
    new_first = beta_first * first_moment + (1.0 - beta_first) * grad
    new_second = beta_second * second_moment + (1.0 - beta_second) * grad * grad
    first_hat = new_first / (1.0 - beta_first**step_count)
    second_hat = new_second / (1.0 - beta_second**step_count)
    step = (first_hat / (jnp.sqrt(second_hat) + adam_epsilon)).astype(bf16)[0]
    opposite = lax.ppermute(step, "rep", along_y(N_Y // 2))
    theirs = lax.ppermute(step, "rep", OTHER_CORE)
    both = jnp.concatenate(
        [jnp.where(first_core, step, theirs), jnp.where(first_core, theirs, step)], axis=0
    )
    near = [lax.ppermute(both, "rep", along_y(i + 1)) for i in range(FAR)]
    other = lax.ppermute(jnp.concatenate([*near, opposite], axis=0), "rep", OTHER_CORE)
    new_weight = fresh_weight(where, label_weight, both, near, opposite, other)

    query_grad = sum_parts(pick, returned)
    return (query_grad, new_weight, new_first, new_second)


def solution(mesh):
    split = Mesh(
        mesh.devices.reshape(mesh.devices.shape[0], N_X, N_Z), ("rep", "x", "z")
    )
    rows = P(("rep", "x", "z"), None)
    labels = P(("x", "z"), None)
    state = P("rep", ("x", "z"), None)
    return jax.shard_map(
        body,
        mesh=split,
        in_specs=(rows, rows, rows, labels, state, state),
        out_specs=(rows, labels, state, state),
        check_vma=False,
    )
```

```python
import jax
import jax.numpy as jnp
from jax import lax
from jax.experimental import pallas as pl
from jax.experimental.pallas import tpu as pltpu
from jax.sharding import Mesh
from jax.sharding import PartitionSpec as P

D = 768
BLOCK = 128
K = 8
CAP = 8
LANES = 128
COLS = D // LANES
N_LAB = 32
N_X = 4
N_Z = 8
Q_DEV = 128
UP = 4
ACROSS = COLS - UP
N_Y = 8
BLK_DEV = 8
SLOTS = BLK_DEV * CAP
CHUNK = COLS * SLOTS
SUB = 64
MIB = 1 << 20
FAR = N_Y // 2 - 1

beta_first = 0.9
beta_second = 0.999
learn_rate = 0.01
adam_epsilon = 1e-08
step_count = 100.0

bf16 = jnp.bfloat16
f32 = jnp.float32


def before_matrix():
    row = lax.broadcasted_iota(jnp.int32, (LANES, LANES), 0)
    col = lax.broadcasted_iota(jnp.int32, (LANES, LANES), 1)
    return (row < col).astype(f32).astype(bf16)


def slot_select(marks):
    named = marks >= 0.0
    earlier = jnp.dot(named.astype(f32).astype(bf16), before_matrix(), preferred_element_type=f32)
    rank = jnp.where(named, earlier, -1.0)
    slot = lax.broadcasted_iota(jnp.int32, (1, CAP, 1), 1).astype(f32)
    return rank[:, None, :] == slot


def begin_kernel(short_ref, pos_ref, rows_ref, up_ref, across_ref):
    info = jnp.concatenate([short_ref[...], pos_ref[...]], axis=0).astype(f32).astype(bf16)
    for c in range(COLS):
        part = rows_ref[:, c * LANES : (c + 1) * LANES]
        if c < UP:
            for z in range(N_Z):
                up_ref[z, c * Q_DEV : (c + 1) * Q_DEV, :] = part
        else:
            across_ref[(c - UP) * Q_DEV : (c - UP + 1) * Q_DEV, :] = part
    for z in range(N_Z):
        up_ref[z, UP * Q_DEV :, :] = info
    across_ref[ACROSS * Q_DEV :, :] = info


def begin(short_t, pos_t, queries):
    return pl.pallas_call(
        begin_kernel,
        out_shape=(
            jax.ShapeDtypeStruct((N_Z, UP * Q_DEV + 2 * K, LANES), bf16),
            jax.ShapeDtypeStruct((ACROSS * Q_DEV + 2 * K, LANES), bf16),
        ),
        cost_estimate=pl.CostEstimate(flops=0, bytes_accessed=1_500_000, transcendentals=0),
        name="begin",
    )(short_t, pos_t, queries)


def marks_of(block, short, positive):
    marks = jnp.full(block.shape, -1.0, f32)
    for k in range(K):
        marks = jnp.where(block == short[k : k + 1, :], positive[k : k + 1, :], marks)
    return marks


def one_hot(marks):
    return slot_select(marks).astype(f32).reshape(marks.shape[0] * CAP, LANES).astype(bf16)


def across_kernel(where_ref, short_ref, pos_ref, *refs):
    *source_refs, out_ref, pick_ref = refs
    x = where_ref[2]
    nblk = N_LAB * BLK_DEV
    every = lax.broadcasted_iota(jnp.int32, (nblk, LANES), 0).astype(f32)
    short, positive = short_ref[...].astype(f32), pos_ref[...].astype(f32)
    pick_ref[...] = one_hot(marks_of(every, short, positive))
    here = N_Z * BLK_DEV
    block = (lax.broadcasted_iota(jnp.int32, (here, LANES), 0) + x * here).astype(f32)
    marks = []
    for ref in source_refs:
        info = ref[ACROSS * Q_DEV :, :].astype(f32)
        marks.append(marks_of(block, info[:K], info[K:]))
    pick = one_hot(jnp.concatenate(marks, axis=0))
    for t, ref in enumerate(source_refs):
        rows = jnp.concatenate(
            [ref[c * Q_DEV : (c + 1) * Q_DEV, :] for c in range(ACROSS)], axis=1
        )
        chosen = jnp.dot(
            pick[t * here * CAP : (t + 1) * here * CAP], rows, preferred_element_type=f32
        ).astype(bf16)
        for z in range(N_Z):
            for c in range(ACROSS):
                out_ref[z, t, c * SLOTS : (c + 1) * SLOTS, :] = chosen[
                    z * SLOTS : (z + 1) * SLOTS, c * LANES : (c + 1) * LANES
                ]


def select_across(where, short_t, pos_t, sources):
    return pl.pallas_call(
        across_kernel,
        in_specs=[pl.BlockSpec(memory_space=pltpu.SMEM)]
        + [pl.BlockSpec(memory_space=pltpu.VMEM)] * (2 + N_X),
        out_shape=(
            jax.ShapeDtypeStruct((N_Z, N_X, ACROSS * SLOTS, LANES), bf16),
            jax.ShapeDtypeStruct((N_LAB * SLOTS, LANES), bf16),
        ),
        cost_estimate=pl.CostEstimate(flops=200_000_000, bytes_accessed=2_000_000, transcendentals=0),
        name="select_across",
    )(where, short_t, pos_t, *sources)


def up_kernel(where_ref, arrived_ref, *out_refs):
    x, z = where_ref[2], where_ref[3]
    index = lax.broadcasted_iota(jnp.int32, (N_X * BLK_DEV, LANES), 0)
    owner_x = (index // BLK_DEV + x) % N_X
    block = (owner_x * (N_Z * BLK_DEV) + z * BLK_DEV + index % BLK_DEV).astype(f32)
    marks = []
    for s in range(N_Z):
        info = arrived_ref[s, UP * Q_DEV :, :].astype(f32)
        marks.append(marks_of(block, info[:K], info[K:]))
    pick = one_hot(jnp.concatenate(marks, axis=0))
    count = N_X * SLOTS
    for s in range(N_Z):
        rows = jnp.concatenate(
            [arrived_ref[s, c * Q_DEV : (c + 1) * Q_DEV, :] for c in range(UP)], axis=1
        )
        chosen = jnp.dot(
            pick[s * count : (s + 1) * count], rows, preferred_element_type=f32
        ).astype(bf16)
        for t in range(N_X):
            for c in range(UP):
                out_refs[t][s, c * SLOTS : (c + 1) * SLOTS, :] = chosen[
                    t * SLOTS : (t + 1) * SLOTS, c * LANES : (c + 1) * LANES
                ]
            out_refs[t][s, UP * SLOTS :, :] = marks[s][t * BLK_DEV : (t + 1) * BLK_DEV].astype(bf16)


def select_up(where, arrived):
    return pl.pallas_call(
        up_kernel,
        in_specs=[
            pl.BlockSpec(memory_space=pltpu.SMEM),
            pl.BlockSpec(memory_space=pltpu.VMEM),
        ],
        out_shape=tuple(
            jax.ShapeDtypeStruct((N_Z, UP * SLOTS + BLK_DEV, LANES), bf16) for _ in range(N_X)
        ),
        cost_estimate=pl.CostEstimate(flops=300_000_000, bytes_accessed=3_000_000, transcendentals=0),
        name="select_up",
    )(where, arrived)


def block_kernel(
    where_ref, a0_ref, a1_ref, a2_ref, a3_ref, b_ref, tiles_ref, back_ref, keep_ref, give_ref, marks_ref, rows_ref
):
    a_refs = (a0_ref, a1_ref, a2_ref, a3_ref)
    x = where_ref[2]
    pair = pl.program_id(0)
    y, core = where_ref[0], where_ref[1]

    @pl.when(pair == 0)
    def _():
        for t in range(N_X):
            marks = a_refs[t][:, UP * SLOTS :, :].astype(f32)
            for b in range(BLK_DEV):
                marks_ref[b, t * N_Z : (t + 1) * N_Z, :] = marks[:, b, :]

    for c in range(COLS):
        group = c if c < UP else c - UP
        at = pl.ds(pl.multiple_of(group * SLOTS + pair * 2 * CAP, 2 * CAP), 2 * CAP)
        for t in range(N_X):
            part = a_refs[t][:, at, :] if c < UP else b_ref[:, t, at, :]
            both = part.astype(f32).reshape(N_Z, 2, CAP, LANES)
            for h in range(2):
                rows_ref[h, t * SLOTS : (t + 1) * SLOTS, c * LANES : (c + 1) * LANES] = (
                    both[:, h].reshape(N_Z * CAP, LANES).astype(bf16)
                )

    label = lax.broadcasted_iota(jnp.int32, (N_LAB * CAP, BLOCK), 1).astype(f32)
    parts = []
    for h in range(2):
        marks = marks_ref[pair * 2 + h]
        held = jnp.where(slot_select(marks), marks[:, None, :] + 1.0, 0.0)
        mark = (jnp.sum(held, axis=2, keepdims=True) - 1.0).reshape(N_LAB * CAP, 1)
        rows = rows_ref[h]
        tile = tiles_ref[h * BLOCK : (h + 1) * BLOCK, :]
        logits = lax.dot_general(rows, tile, (((1,), (1,)), ((), ())), preferred_element_type=f32)
        slopes = (jax.nn.sigmoid(logits) - (label == mark).astype(f32)).astype(bf16)
        parts.append(jnp.dot(slopes, tile, preferred_element_type=f32))
        grad = lax.dot_general(slopes, rows, (((0,), (0,)), ((), ())), preferred_element_type=f32)
        ahead = lax.rem(pair * 2 + h - y + N_Y, N_Y)
        halved = lax.rem(ahead, N_Y // 2) == 0
        first = ahead < N_Y // 2
        unit = jnp.where(first, ahead, N_Y - ahead) * 2 - 2
        own = jnp.where(first, 0, 1) == core
        for i in range(2):
            at = jnp.where(halved, jnp.where(first, N_Y - 1, N_Y - 2), unit + i)
            kept = jnp.where(halved, core == i, own)

            @pl.when(kept)
            def _():
                keep_ref[at] = grad[i * SUB : (i + 1) * SUB]

            @pl.when(jnp.logical_not(kept))
            def _():
                give_ref[at] = grad[i * SUB : (i + 1) * SUB]

    for c in range(COLS):
        cols = slice(c * LANES, (c + 1) * LANES)
        both = jnp.stack([p[:, cols].reshape(N_LAB, CAP, LANES) for p in parts], axis=1)
        both = both.reshape(N_LAB, 2 * CAP, LANES).astype(bf16)
        for t in range(N_X):
            source_x = lax.rem(x - t + N_X, N_X)
            back_ref[pl.ds(source_x * N_Z, N_Z), c, 0] = both[t * N_Z : (t + 1) * N_Z]


def label_blocks(where, up, across, label_weight):
    pairs = BLK_DEV // 2
    return pl.pallas_call(
        block_kernel,
        grid=(pairs,),
        in_specs=[
            pl.BlockSpec(memory_space=pltpu.SMEM),
        ]
        + [pl.BlockSpec((N_Z, UP * SLOTS + BLK_DEV, LANES), lambda p: (0, 0, 0))] * N_X
        + [
            pl.BlockSpec((N_Z, N_X, ACROSS * SLOTS, LANES), lambda p: (0, 0, 0, 0)),
            pl.BlockSpec((2 * BLOCK, D), lambda p: (p, 0)),
        ],
        out_specs=[
            pl.BlockSpec((N_LAB, COLS, 1, 2 * CAP, LANES), lambda p: (0, 0, p, 0, 0)),
            pl.BlockSpec((N_Y, SUB, D), lambda p: (0, 0, 0)),
            pl.BlockSpec((N_Y, SUB, D), lambda p: (0, 0, 0)),
        ],
        out_shape=(
            jax.ShapeDtypeStruct((N_LAB, COLS, pairs, 2 * CAP, LANES), bf16),
            jax.ShapeDtypeStruct((BLK_DEV, SUB, D), f32),
            jax.ShapeDtypeStruct((BLK_DEV, SUB, D), f32),
        ),
        scratch_shapes=[
            pltpu.VMEM((BLK_DEV, N_LAB, LANES), f32),
            pltpu.VMEM((2, N_LAB * CAP, D), bf16),
        ],
        cost_estimate=pl.CostEstimate(
            flops=1_210_000_000, bytes_accessed=11_000_000, transcendentals=300_000
        ),
        name="label_blocks",
    )(where, *up, across, label_weight)


def sum_kernel(pick_ref, back_ref, out_ref):
    step = pl.program_id(0)
    groups = back_ref.shape[0]
    pick = pick_ref[...]
    cols = []
    for c in range(COLS):
        part = back_ref[:, c * SLOTS : (c + 1) * SLOTS, :].reshape(groups * SLOTS, LANES)
        cols.append(part)
    parts = jnp.concatenate(cols, axis=1)
    total = lax.dot_general(pick, parts, (((0,), (0,)), ((), ())), preferred_element_type=f32)

    @pl.when(step == 0)
    def _():
        out_ref[...] = total

    @pl.when(step > 0)
    def _():
        out_ref[...] += total


def sum_parts(pick, back):
    steps = 4
    groups = N_LAB // steps
    return pl.pallas_call(
        sum_kernel,
        grid=(steps,),
        in_specs=[
            pl.BlockSpec((groups * SLOTS, LANES), lambda g: (g, 0)),
            pl.BlockSpec((groups, CHUNK, LANES), lambda g: (g, 0, 0)),
        ],
        out_specs=pl.BlockSpec((LANES, D), lambda g: (0, 0)),
        out_shape=jax.ShapeDtypeStruct((LANES, D), f32),
        cost_estimate=pl.CostEstimate(flops=400_000_000, bytes_accessed=4_000_000, transcendentals=0),
        name="sum_parts",
        compiler_params=pltpu.CompilerParams(vmem_limit_bytes=16 * MIB),
    )(pick, back)


def split_kernel(keep_ref, got_ref, *out_refs):
    for s in range(FAR):
        for i in range(2):
            u = 2 * s + i
            out_refs[s][i * SUB : (i + 1) * SUB, :] = (keep_ref[u] + got_ref[u]).astype(bf16)
    out_refs[FAR][...] = (keep_ref[2 * FAR] + got_ref[2 * FAR]).astype(bf16)
    out_refs[FAR + 1][...] = keep_ref[2 * FAR + 1] + got_ref[2 * FAR + 1]


def split_by_y(keep, got):
    return pl.pallas_call(
        split_kernel,
        out_shape=tuple(jax.ShapeDtypeStruct((BLOCK, D), bf16) for _ in range(FAR))
        + (jax.ShapeDtypeStruct((SUB, D), bf16), jax.ShapeDtypeStruct((SUB, D), f32)),
        cost_estimate=pl.CostEstimate(flops=400_000, bytes_accessed=4_000_000, transcendentals=0),
        name="split_by_y",
    )(keep, got)


def weight_block(tile_ref, out_ref, step):
    out_ref[...] = tile_ref[...].astype(f32) - learn_rate * step.astype(f32)


def near_kernel(where_ref, tile_ref, both_ref, one_ref, two_ref, three_ref, out_ref):
    step = pl.program_id(0)
    for i, ref in enumerate((both_ref, one_ref, two_ref, three_ref)):

        @pl.when(step == i)
        def _():
            weight_block(tile_ref, out_ref, ref[...])


def far_kernel(where_ref, tile_ref, mine_ref, other_ref, begun_ref, out_ref):
    step = pl.program_id(0)
    core = where_ref[1]

    @pl.when(step == 0)
    def _():
        mine = mine_ref[...].astype(f32)
        other = other_ref[FAR * BLOCK :, :].astype(f32)
        low = jnp.where(core == 0, mine, other)
        high = jnp.where(core == 0, other, mine)
        weight_block(tile_ref, out_ref, jnp.concatenate([low, high], axis=0))

    for i in range(FAR):

        @pl.when(step == i + 1)
        def _():
            weight_block(tile_ref, out_ref, other_ref[i * BLOCK : (i + 1) * BLOCK, :])


def way(where_ref):
    return 1 - 2 * where_ref[1]


def near_tile(t, where_ref):
    return (lax.rem(where_ref[0] - way(where_ref) * t + N_Y, N_Y), 0)


def far_tile(t, where_ref):
    ahead = jnp.where(t == 0, N_Y // 2, way(where_ref) * t)
    return (lax.rem(where_ref[0] + ahead + N_Y, N_Y), 0)


def whole(shape):
    return pl.BlockSpec(shape, lambda t, where_ref: (0,) * len(shape))


def fresh_weight(where, label_weight, both, near, opposite, other):
    out_shape = jax.ShapeDtypeStruct((N_Y * BLOCK, D), f32)
    cost = pl.CostEstimate(flops=800_000, bytes_accessed=3_200_000, transcendentals=0)
    begun = pl.pallas_call(
        near_kernel,
        grid_spec=pltpu.PrefetchScalarGridSpec(
            num_scalar_prefetch=1,
            grid=(N_Y // 2,),
            in_specs=[pl.BlockSpec((BLOCK, D), near_tile)] + [whole((BLOCK, D))] * 4,
            out_specs=pl.BlockSpec((BLOCK, D), near_tile),
        ),
        out_shape=out_shape,
        cost_estimate=cost,
        name="near_weight",
        compiler_params=pltpu.CompilerParams(vmem_limit_bytes=10 * MIB),
    )(where, label_weight, both, *near)
    return pl.pallas_call(
        far_kernel,
        grid_spec=pltpu.PrefetchScalarGridSpec(
            num_scalar_prefetch=1,
            grid=(N_Y // 2,),
            in_specs=[
                pl.BlockSpec((BLOCK, D), far_tile),
                whole((SUB, D)),
                whole((FAR * BLOCK + SUB, D)),
                pl.BlockSpec(memory_space=pl.ANY),
            ],
            out_specs=pl.BlockSpec((BLOCK, D), far_tile),
        ),
        out_shape=out_shape,
        input_output_aliases={4: 0},
        cost_estimate=cost,
        name="far_weight",
        compiler_params=pltpu.CompilerParams(vmem_limit_bytes=10 * MIB),
    )(where, label_weight, opposite, other, begun)


def along_y(shift):
    return [(y * 2 + c, ((y + (1 - 2 * c) * shift) % N_Y) * 2 + c) for y in range(N_Y) for c in range(2)]


OTHER_CORE = [(r, r ^ 1) for r in range(2 * N_Y)]


def along_x(shift):
    return [(x, (x + shift) % N_X) for x in range(N_X)]


def body(queries, shortlist, positive, label_weight, first_moment, second_moment):
    rep = lax.axis_index("rep")
    where = jnp.stack([rep // 2, rep % 2, lax.axis_index("x"), lax.axis_index("z")])
    where = where.astype(jnp.int32)
    short_t, pos_t = shortlist.T, positive.T
    up, across = begin(short_t, pos_t, queries)
    up = lax.all_to_all(up, "z", split_axis=0, concat_axis=0, tiled=True)
    sources = [across] + [lax.ppermute(across, "x", along_x(t)) for t in range(1, N_X)]
    across, pick = select_across(where, short_t, pos_t, sources)
    across = lax.all_to_all(across, "z", split_axis=0, concat_axis=0, tiled=True)
    up = select_up(where, up)
    up = [up[0]] + [lax.ppermute(up[t], "x", along_x(t)) for t in range(1, N_X)]
    back, keep, give = label_blocks(where, up, across, label_weight)
    back = back.reshape(N_LAB, CHUNK, LANES)
    returned = lax.all_to_all(back, ("x", "z"), split_axis=0, concat_axis=0, tiled=True)
    got = lax.ppermute(give, "rep", OTHER_CORE)
    *sides, opposite, grad = split_by_y(keep, got)
    side = jnp.zeros((BLOCK, D), f32)
    for i, share in enumerate(sides):
        side = side + lax.ppermute(share, "rep", along_y(i + 1)).astype(f32)
    first_core = where[1] == 0
    far = lax.ppermute(opposite, "rep", along_y(N_Y // 2)).astype(f32)
    low = side[:SUB] + jnp.where(first_core, far, 0.0)
    high = side[SUB:] + jnp.where(first_core, 0.0, far)
    grad = grad + jnp.where(first_core, low, high)
    grad = grad + lax.ppermute(jnp.where(first_core, high, low), "rep", OTHER_CORE)
    grad = grad[None]
    new_first = beta_first * first_moment + (1.0 - beta_first) * grad
    new_second = beta_second * second_moment + (1.0 - beta_second) * grad * grad
    first_hat = new_first / (1.0 - beta_first**step_count)
    second_hat = new_second / (1.0 - beta_second**step_count)
    step = (first_hat / (jnp.sqrt(second_hat) + adam_epsilon)).astype(bf16)[0]
    opposite = lax.ppermute(step, "rep", along_y(N_Y // 2))
    theirs = lax.ppermute(step, "rep", OTHER_CORE)
    both = jnp.concatenate(
        [jnp.where(first_core, step, theirs), jnp.where(first_core, theirs, step)], axis=0
    )
    near = [lax.ppermute(both, "rep", along_y(i + 1)) for i in range(FAR)]
    other = lax.ppermute(jnp.concatenate([*near, opposite], axis=0), "rep", OTHER_CORE)
    new_weight = fresh_weight(where, label_weight, both, near, opposite, other)

    query_grad = sum_parts(pick, returned)
    return (query_grad, new_weight, new_first, new_second)


def solution(mesh):
    split = Mesh(
        mesh.devices.reshape(mesh.devices.shape[0], N_X, N_Z), ("rep", "x", "z")
    )
    rows = P(("rep", "x", "z"), None)
    labels = P(("x", "z"), None)
    state = P("rep", ("x", "z"), None)
    return jax.shard_map(
        body,
        mesh=split,
        in_specs=(rows, rows, rows, labels, state, state),
        out_specs=(rows, labels, state, state),
        check_vma=False,
    )
```

```python
import jax
import jax.numpy as jnp
from jax import lax
from jax.experimental import pallas as pl
from jax.experimental.pallas import tpu as pltpu
from jax.sharding import Mesh
from jax.sharding import PartitionSpec as P

D = 768
BLOCK = 128
K = 8
CAP = 8
LANES = 128
COLS = D // LANES
N_LAB = 32
N_X = 4
N_Z = 8
Q_DEV = 128
UP = 4
ACROSS = COLS - UP
N_Y = 8
BLK_DEV = 8
SLOTS = BLK_DEV * CAP
CHUNK = COLS * SLOTS
SUB = 64
MIB = 1 << 20
FAR = N_Y // 2 - 1

beta_first = 0.9
beta_second = 0.999
learn_rate = 0.01
adam_epsilon = 1e-08
step_count = 100.0

bf16 = jnp.bfloat16
f32 = jnp.float32


def before_matrix():
    row = lax.broadcasted_iota(jnp.int32, (LANES, LANES), 0)
    col = lax.broadcasted_iota(jnp.int32, (LANES, LANES), 1)
    return (row < col).astype(f32).astype(bf16)


def slot_select(marks):
    named = marks >= 0.0
    earlier = jnp.dot(named.astype(f32).astype(bf16), before_matrix(), preferred_element_type=f32)
    rank = jnp.where(named, earlier, -1.0)
    slot = lax.broadcasted_iota(jnp.int32, (1, CAP, 1), 1).astype(f32)
    return rank[:, None, :] == slot


def begin_kernel(short_ref, pos_ref, rows_ref, up_ref, across_ref):
    info = jnp.concatenate([short_ref[...], pos_ref[...]], axis=0).astype(f32).astype(bf16)
    for c in range(COLS):
        part = rows_ref[:, c * LANES : (c + 1) * LANES]
        if c < UP:
            for z in range(N_Z):
                up_ref[z, c * Q_DEV : (c + 1) * Q_DEV, :] = part
        else:
            across_ref[(c - UP) * Q_DEV : (c - UP + 1) * Q_DEV, :] = part
    for z in range(N_Z):
        up_ref[z, UP * Q_DEV :, :] = info
    across_ref[ACROSS * Q_DEV :, :] = info


def begin(short_t, pos_t, queries):
    return pl.pallas_call(
        begin_kernel,
        out_shape=(
            jax.ShapeDtypeStruct((N_Z, UP * Q_DEV + 2 * K, LANES), bf16),
            jax.ShapeDtypeStruct((ACROSS * Q_DEV + 2 * K, LANES), bf16),
        ),
        cost_estimate=pl.CostEstimate(flops=0, bytes_accessed=1_500_000, transcendentals=0),
        name="begin",
    )(short_t, pos_t, queries)


def marks_of(block, short, positive):
    marks = jnp.full(block.shape, -1.0, f32)
    for k in range(K):
        marks = jnp.where(block == short[k : k + 1, :], positive[k : k + 1, :], marks)
    return marks


def one_hot(marks):
    return slot_select(marks).astype(f32).reshape(marks.shape[0] * CAP, LANES).astype(bf16)


def across_kernel(where_ref, short_ref, pos_ref, *refs):
    *source_refs, out_ref, pick_ref = refs
    x = where_ref[2]
    nblk = N_LAB * BLK_DEV
    every = lax.broadcasted_iota(jnp.int32, (nblk, LANES), 0).astype(f32)
    short, positive = short_ref[...].astype(f32), pos_ref[...].astype(f32)
    pick_ref[...] = one_hot(marks_of(every, short, positive))
    here = N_Z * BLK_DEV
    block = (lax.broadcasted_iota(jnp.int32, (here, LANES), 0) + x * here).astype(f32)
    marks = []
    for ref in source_refs:
        info = ref[ACROSS * Q_DEV :, :].astype(f32)
        marks.append(marks_of(block, info[:K], info[K:]))
    pick = one_hot(jnp.concatenate(marks, axis=0))
    for t, ref in enumerate(source_refs):
        rows = jnp.concatenate(
            [ref[c * Q_DEV : (c + 1) * Q_DEV, :] for c in range(ACROSS)], axis=1
        )
        chosen = jnp.dot(
            pick[t * here * CAP : (t + 1) * here * CAP], rows, preferred_element_type=f32
        ).astype(bf16)
        for z in range(N_Z):
            for c in range(ACROSS):
                out_ref[z, t, c * SLOTS : (c + 1) * SLOTS, :] = chosen[
                    z * SLOTS : (z + 1) * SLOTS, c * LANES : (c + 1) * LANES
                ]


def select_across(where, short_t, pos_t, sources):
    return pl.pallas_call(
        across_kernel,
        in_specs=[pl.BlockSpec(memory_space=pltpu.SMEM)]
        + [pl.BlockSpec(memory_space=pltpu.VMEM)] * (2 + N_X),
        out_shape=(
            jax.ShapeDtypeStruct((N_Z, N_X, ACROSS * SLOTS, LANES), bf16),
            jax.ShapeDtypeStruct((N_LAB * SLOTS, LANES), bf16),
        ),
        cost_estimate=pl.CostEstimate(flops=200_000_000, bytes_accessed=2_000_000, transcendentals=0),
        name="select_across",
    )(where, short_t, pos_t, *sources)


def up_kernel(where_ref, arrived_ref, *out_refs):
    x, z = where_ref[2], where_ref[3]
    index = lax.broadcasted_iota(jnp.int32, (N_X * BLK_DEV, LANES), 0)
    owner_x = (index // BLK_DEV + x) % N_X
    block = (owner_x * (N_Z * BLK_DEV) + z * BLK_DEV + index % BLK_DEV).astype(f32)
    marks = []
    for s in range(N_Z):
        info = arrived_ref[s, UP * Q_DEV :, :].astype(f32)
        marks.append(marks_of(block, info[:K], info[K:]))
    pick = one_hot(jnp.concatenate(marks, axis=0))
    count = N_X * SLOTS
    for s in range(N_Z):
        rows = jnp.concatenate(
            [arrived_ref[s, c * Q_DEV : (c + 1) * Q_DEV, :] for c in range(UP)], axis=1
        )
        chosen = jnp.dot(
            pick[s * count : (s + 1) * count], rows, preferred_element_type=f32
        ).astype(bf16)
        for t in range(N_X):
            for c in range(UP):
                out_refs[t][s, c * SLOTS : (c + 1) * SLOTS, :] = chosen[
                    t * SLOTS : (t + 1) * SLOTS, c * LANES : (c + 1) * LANES
                ]
            out_refs[t][s, UP * SLOTS :, :] = marks[s][t * BLK_DEV : (t + 1) * BLK_DEV].astype(bf16)


def select_up(where, arrived):
    return pl.pallas_call(
        up_kernel,
        in_specs=[
            pl.BlockSpec(memory_space=pltpu.SMEM),
            pl.BlockSpec(memory_space=pltpu.VMEM),
        ],
        out_shape=tuple(
            jax.ShapeDtypeStruct((N_Z, UP * SLOTS + BLK_DEV, LANES), bf16) for _ in range(N_X)
        ),
        cost_estimate=pl.CostEstimate(flops=300_000_000, bytes_accessed=3_000_000, transcendentals=0),
        name="select_up",
    )(where, arrived)


def block_kernel(
    where_ref, a0_ref, a1_ref, a2_ref, a3_ref, b_ref, tiles_ref, back_ref, keep_ref, give_ref, marks_ref, rows_ref
):
    a_refs = (a0_ref, a1_ref, a2_ref, a3_ref)
    x = where_ref[2]
    pair = pl.program_id(0)
    y, core = where_ref[0], where_ref[1]

    @pl.when(pair == 0)
    def _():
        for t in range(N_X):
            marks = a_refs[t][:, UP * SLOTS :, :].astype(f32)
            for b in range(BLK_DEV):
                marks_ref[b, t * N_Z : (t + 1) * N_Z, :] = marks[:, b, :]

    for c in range(COLS):
        group = c if c < UP else c - UP
        at = pl.ds(pl.multiple_of(group * SLOTS + pair * 2 * CAP, 2 * CAP), 2 * CAP)
        for t in range(N_X):
            part = a_refs[t][:, at, :] if c < UP else b_ref[:, t, at, :]
            both = part.astype(f32).reshape(N_Z, 2, CAP, LANES)
            for h in range(2):
                rows_ref[h, t * SLOTS : (t + 1) * SLOTS, c * LANES : (c + 1) * LANES] = (
                    both[:, h].reshape(N_Z * CAP, LANES).astype(bf16)
                )

    label = lax.broadcasted_iota(jnp.int32, (N_LAB * CAP, BLOCK), 1).astype(f32)
    parts = []
    for h in range(2):
        marks = marks_ref[pair * 2 + h]
        held = jnp.where(slot_select(marks), marks[:, None, :] + 1.0, 0.0)
        mark = (jnp.sum(held, axis=2, keepdims=True) - 1.0).reshape(N_LAB * CAP, 1)
        rows = rows_ref[h]
        tile = tiles_ref[h * BLOCK : (h + 1) * BLOCK, :]
        logits = lax.dot_general(rows, tile, (((1,), (1,)), ((), ())), preferred_element_type=f32)
        slopes = (jax.nn.sigmoid(logits) - (label == mark).astype(f32)).astype(bf16)
        parts.append(jnp.dot(slopes, tile, preferred_element_type=f32))
        grad = lax.dot_general(slopes, rows, (((0,), (0,)), ((), ())), preferred_element_type=f32)
        ahead = lax.rem(pair * 2 + h - y + N_Y, N_Y)
        halved = lax.rem(ahead, N_Y // 2) == 0
        first = ahead < N_Y // 2
        unit = jnp.where(first, ahead, N_Y - ahead) * 2 - 2
        own = jnp.where(first, 0, 1) == core
        for i in range(2):
            at = jnp.where(halved, jnp.where(first, N_Y - 1, N_Y - 2), unit + i)
            kept = jnp.where(halved, core == i, own)

            @pl.when(kept)
            def _():
                keep_ref[at] = grad[i * SUB : (i + 1) * SUB]

            @pl.when(jnp.logical_not(kept))
            def _():
                give_ref[at] = grad[i * SUB : (i + 1) * SUB]

    for c in range(COLS):
        cols = slice(c * LANES, (c + 1) * LANES)
        both = jnp.stack([p[:, cols].reshape(N_LAB, CAP, LANES) for p in parts], axis=1)
        both = both.reshape(N_LAB, 2 * CAP, LANES).astype(bf16)
        for t in range(N_X):
            source_x = lax.rem(x - t + N_X, N_X)
            back_ref[pl.ds(source_x * N_Z, N_Z), c, 0] = both[t * N_Z : (t + 1) * N_Z]


def label_blocks(where, up, across, label_weight):
    pairs = BLK_DEV // 2
    return pl.pallas_call(
        block_kernel,
        grid=(pairs,),
        in_specs=[
            pl.BlockSpec(memory_space=pltpu.SMEM),
        ]
        + [pl.BlockSpec((N_Z, UP * SLOTS + BLK_DEV, LANES), lambda p: (0, 0, 0))] * N_X
        + [
            pl.BlockSpec((N_Z, N_X, ACROSS * SLOTS, LANES), lambda p: (0, 0, 0, 0)),
            pl.BlockSpec((2 * BLOCK, D), lambda p: (p, 0)),
        ],
        out_specs=[
            pl.BlockSpec((N_LAB, COLS, 1, 2 * CAP, LANES), lambda p: (0, 0, p, 0, 0)),
            pl.BlockSpec((N_Y, SUB, D), lambda p: (0, 0, 0)),
            pl.BlockSpec((N_Y, SUB, D), lambda p: (0, 0, 0)),
        ],
        out_shape=(
            jax.ShapeDtypeStruct((N_LAB, COLS, pairs, 2 * CAP, LANES), bf16),
            jax.ShapeDtypeStruct((BLK_DEV, SUB, D), f32),
            jax.ShapeDtypeStruct((BLK_DEV, SUB, D), f32),
        ),
        scratch_shapes=[
            pltpu.VMEM((BLK_DEV, N_LAB, LANES), f32),
            pltpu.VMEM((2, N_LAB * CAP, D), bf16),
        ],
        cost_estimate=pl.CostEstimate(
            flops=1_210_000_000, bytes_accessed=11_000_000, transcendentals=300_000
        ),
        name="label_blocks",
        compiler_params=pltpu.CompilerParams(vmem_limit_bytes=50 * MIB),
    )(where, *up, across, label_weight)


def sum_kernel(pick_ref, back_ref, out_ref):
    step = pl.program_id(0)
    groups = back_ref.shape[0]
    pick = pick_ref[...]
    cols = []
    for c in range(COLS):
        part = back_ref[:, c * SLOTS : (c + 1) * SLOTS, :].reshape(groups * SLOTS, LANES)
        cols.append(part)
    parts = jnp.concatenate(cols, axis=1)
    total = lax.dot_general(pick, parts, (((0,), (0,)), ((), ())), preferred_element_type=f32)

    @pl.when(step == 0)
    def _():
        out_ref[...] = total

    @pl.when(step > 0)
    def _():
        out_ref[...] += total


def sum_parts(pick, back):
    steps = 4
    groups = N_LAB // steps
    return pl.pallas_call(
        sum_kernel,
        grid=(steps,),
        in_specs=[
            pl.BlockSpec((groups * SLOTS, LANES), lambda g: (g, 0)),
            pl.BlockSpec((groups, CHUNK, LANES), lambda g: (g, 0, 0)),
        ],
        out_specs=pl.BlockSpec((LANES, D), lambda g: (0, 0)),
        out_shape=jax.ShapeDtypeStruct((LANES, D), f32),
        cost_estimate=pl.CostEstimate(flops=400_000_000, bytes_accessed=4_000_000, transcendentals=0),
        name="sum_parts",
        compiler_params=pltpu.CompilerParams(vmem_limit_bytes=57 * MIB),
    )(pick, back)


def split_kernel(keep_ref, got_ref, *out_refs):
    for s in range(FAR):
        for i in range(2):
            u = 2 * s + i
            out_refs[s][i * SUB : (i + 1) * SUB, :] = (keep_ref[u] + got_ref[u]).astype(bf16)
    out_refs[FAR][...] = (keep_ref[2 * FAR] + got_ref[2 * FAR]).astype(bf16)
    out_refs[FAR + 1][...] = keep_ref[2 * FAR + 1] + got_ref[2 * FAR + 1]


def split_by_y(keep, got):
    return pl.pallas_call(
        split_kernel,
        out_shape=tuple(jax.ShapeDtypeStruct((BLOCK, D), bf16) for _ in range(FAR))
        + (jax.ShapeDtypeStruct((SUB, D), bf16), jax.ShapeDtypeStruct((SUB, D), f32)),
        cost_estimate=pl.CostEstimate(flops=400_000, bytes_accessed=4_000_000, transcendentals=0),
        name="split_by_y",
    )(keep, got)


def weight_block(tile_ref, out_ref, step):
    out_ref[...] = tile_ref[...].astype(f32) - learn_rate * step.astype(f32)


def near_kernel(where_ref, tile_ref, both_ref, one_ref, two_ref, three_ref, out_ref):
    step = pl.program_id(0)
    for i, ref in enumerate((both_ref, one_ref, two_ref, three_ref)):

        @pl.when(step == i)
        def _():
            weight_block(tile_ref, out_ref, ref[...])


def far_kernel(where_ref, tile_ref, mine_ref, other_ref, begun_ref, out_ref):
    step = pl.program_id(0)
    core = where_ref[1]

    @pl.when(step == 0)
    def _():
        mine = mine_ref[...].astype(f32)
        other = other_ref[FAR * BLOCK :, :].astype(f32)
        low = jnp.where(core == 0, mine, other)
        high = jnp.where(core == 0, other, mine)
        weight_block(tile_ref, out_ref, jnp.concatenate([low, high], axis=0))

    for i in range(FAR):

        @pl.when(step == i + 1)
        def _():
            weight_block(tile_ref, out_ref, other_ref[i * BLOCK : (i + 1) * BLOCK, :])


def way(where_ref):
    return 1 - 2 * where_ref[1]


def near_tile(t, where_ref):
    return (lax.rem(where_ref[0] - way(where_ref) * t + N_Y, N_Y), 0)


def far_tile(t, where_ref):
    ahead = jnp.where(t == 0, N_Y // 2, way(where_ref) * t)
    return (lax.rem(where_ref[0] + ahead + N_Y, N_Y), 0)


def whole(shape):
    return pl.BlockSpec(shape, lambda t, where_ref: (0,) * len(shape))


def fresh_weight(where, label_weight, both, near, opposite, other):
    out_shape = jax.ShapeDtypeStruct((N_Y * BLOCK, D), f32)
    cost = pl.CostEstimate(flops=800_000, bytes_accessed=3_200_000, transcendentals=0)
    begun = pl.pallas_call(
        near_kernel,
        grid_spec=pltpu.PrefetchScalarGridSpec(
            num_scalar_prefetch=1,
            grid=(N_Y // 2,),
            in_specs=[pl.BlockSpec((BLOCK, D), near_tile)] + [whole((BLOCK, D))] * 4,
            out_specs=pl.BlockSpec((BLOCK, D), near_tile),
        ),
        out_shape=out_shape,
        cost_estimate=cost,
        name="near_weight",
        compiler_params=pltpu.CompilerParams(vmem_limit_bytes=10 * MIB),
    )(where, label_weight, both, *near)
    return pl.pallas_call(
        far_kernel,
        grid_spec=pltpu.PrefetchScalarGridSpec(
            num_scalar_prefetch=1,
            grid=(N_Y // 2,),
            in_specs=[
                pl.BlockSpec((BLOCK, D), far_tile),
                whole((SUB, D)),
                whole((FAR * BLOCK + SUB, D)),
                pl.BlockSpec(memory_space=pl.ANY),
            ],
            out_specs=pl.BlockSpec((BLOCK, D), far_tile),
        ),
        out_shape=out_shape,
        input_output_aliases={4: 0},
        cost_estimate=cost,
        name="far_weight",
        compiler_params=pltpu.CompilerParams(vmem_limit_bytes=10 * MIB),
    )(where, label_weight, opposite, other, begun)


def along_y(shift):
    return [(y * 2 + c, ((y + (1 - 2 * c) * shift) % N_Y) * 2 + c) for y in range(N_Y) for c in range(2)]


OTHER_CORE = [(r, r ^ 1) for r in range(2 * N_Y)]


def along_x(shift):
    return [(x, (x + shift) % N_X) for x in range(N_X)]


def body(queries, shortlist, positive, label_weight, first_moment, second_moment):
    rep = lax.axis_index("rep")
    where = jnp.stack([rep // 2, rep % 2, lax.axis_index("x"), lax.axis_index("z")])
    where = where.astype(jnp.int32)
    short_t, pos_t = shortlist.T, positive.T
    up, across = begin(short_t, pos_t, queries)
    up = lax.all_to_all(up, "z", split_axis=0, concat_axis=0, tiled=True)
    sources = [across] + [lax.ppermute(across, "x", along_x(t)) for t in range(1, N_X)]
    across, pick = select_across(where, short_t, pos_t, sources)
    up = select_up(where, up)
    opposite = lax.ppermute(up[2], "x", along_x(2))
    across = lax.all_to_all(across, "z", split_axis=0, concat_axis=0, tiled=True)
    beside = [lax.ppermute(up[t], "x", along_x(t)) for t in (1, 3)]
    up = [up[0], beside[0], opposite, beside[1]]
    back, keep, give = label_blocks(where, up, across, label_weight)
    back = back.reshape(N_LAB, CHUNK, LANES)
    returned = lax.all_to_all(back, ("x", "z"), split_axis=0, concat_axis=0, tiled=True)
    got = lax.ppermute(give, "rep", OTHER_CORE)
    *sides, opposite, grad = split_by_y(keep, got)
    side = jnp.zeros((BLOCK, D), f32)
    for i, share in enumerate(sides):
        side = side + lax.ppermute(share, "rep", along_y(i + 1)).astype(f32)
    first_core = where[1] == 0
    far = lax.ppermute(opposite, "rep", along_y(N_Y // 2)).astype(f32)
    low = side[:SUB] + jnp.where(first_core, far, 0.0)
    high = side[SUB:] + jnp.where(first_core, 0.0, far)
    grad = grad + jnp.where(first_core, low, high)
    grad = grad + lax.ppermute(jnp.where(first_core, high, low), "rep", OTHER_CORE)
    grad = grad[None]
    new_first = beta_first * first_moment + (1.0 - beta_first) * grad
    new_second = beta_second * second_moment + (1.0 - beta_second) * grad * grad
    first_hat = new_first / (1.0 - beta_first**step_count)
    second_hat = new_second / (1.0 - beta_second**step_count)
    step = (first_hat / (jnp.sqrt(second_hat) + adam_epsilon)).astype(bf16)[0]
    opposite = lax.ppermute(step, "rep", along_y(N_Y // 2))
    theirs = lax.ppermute(step, "rep", OTHER_CORE)
    both = jnp.concatenate(
        [jnp.where(first_core, step, theirs), jnp.where(first_core, theirs, step)], axis=0
    )
    near = [lax.ppermute(both, "rep", along_y(i + 1)) for i in range(FAR)]
    other = lax.ppermute(jnp.concatenate([*near, opposite], axis=0), "rep", OTHER_CORE)
    new_weight = fresh_weight(where, label_weight, both, near, opposite, other)

    query_grad = sum_parts(pick, returned)
    return (query_grad, new_weight, new_first, new_second)


def solution(mesh):
    split = Mesh(
        mesh.devices.reshape(mesh.devices.shape[0], N_X, N_Z), ("rep", "x", "z")
    )
    rows = P(("rep", "x", "z"), None)
    labels = P(("x", "z"), None)
    state = P("rep", ("x", "z"), None)
    return jax.shard_map(
        body,
        mesh=split,
        in_specs=(rows, rows, rows, labels, state, state),
        out_specs=(rows, labels, state, state),
        check_vma=False,
    )
```
